32 devices in a mesh: req: 8 (over z, y), kv: 4 (over x, core).
Axes of the slice: x: 2, y: 2, z: 4, core: 2. Of those that a mesh axis runs over, the one named last changes fastest.
Arguments:
- tokens: bfloat16 [8, 128, 2880], P('req'), may hold values from -6 to 6
- attn_gain: float32 [2880], replicated, may hold values from 0.1 to 1.9
- w_qkv: bfloat16 [2880, 5120], P(None, 'kv'), may hold values from -0.109375 to 0.109375
- sink_logits: float32 [64], P('kv'), may hold values from 0 to 10
- w_out: bfloat16 [4096, 2880], P('kv'), may hold values from -0.09375 to 0.09375
- kv_cache: bfloat16 [1024, 128, 1024], P('req', None, 'kv'), may hold values from -102 to 102
- page_table: int32 [8, 128], P('req'), may hold values from 0 to 127, each once within a row
- cache_lengths: int32 [8], P('req'), may hold values from 0 to 16384, as said below
- moe_gain: float32 [2880], replicated, may hold values from 0.1 to 1.9
- routes: int32 [8, 128, 4], P('req'), may hold values from 0 to 15, all different within a row; in each aligned block of 32 rows (0 to 31, 32 to 63, ..., all dimensions but the last counted through in order) at most 12 rows name the same one
- gate_weights: float32 [8, 128, 4], P('req'), may hold values from 0.1 to 0.7
- w_gate_up: bfloat16 [16, 2, 2880, 2880], P('req', None, None, 'kv'), may hold values from -0.109375 to 0.109375
- w_down: bfloat16 [16, 2880, 2880], P('req', 'kv'), may hold values from -0.109375 to 0.109375
Outputs:
- layer_out: bfloat16 [8, 128, 2880], P('req', 'kv')
The draws below stay inside these ranges and needn't reach their ends.
Inputs may be any that keep to these rules, and one draw needn't show every extreme that they name: `routes`: each token names 4 different experts. In each aligned block of 32 tokens (requests first, then new tokens) no expert is named by more than 12 tokens, and some block reaches 12. `page_table`: each row names every one of its request's 128 pages once. `cache_lengths`: some request's cache is full.
All inputs are finite; a program needn't handle non-finite values.
Results may differ from the reference program's by a relative error of at most 0.014.
Values may be sent and summed in bfloat16 or wider, within the bound.
A program may use at most 192 MiB of HBM per device.

```python
import math
import jax
import jax.numpy as jnp
import numpy as np
from jax import lax

D = 2880
QH = 64
KVH = 8
HD = 64
FF = 2880
TOP = 4
PAGE = 128
NEW_TOK = 128
PAGES_DEV = 128
GROUP = 8
EXPERTS = 16
REQS = 8
POOL = 1024
CTX = 16384
ROWS_DEV = 32
CAP = 12
N_REQ = 8
N_KV = 4


def draw_kv_cache(key, part):
    base_key = jax.random.fold_in(key, 11)
    entries = jnp.clip(jax.random.normal(base_key, (POOL, PAGE, KVH, 2, HD), jnp.float32), -4.0, 4.0)
    return entries.reshape(POOL, PAGE, KVH * 2 * HD).astype(jnp.bfloat16)


def draw_cache_lengths(key, part):
    value_key = jax.random.fold_in(key, 21)
    place_key = jax.random.fold_in(key, 22)
    drawn = jax.random.randint(value_key, (REQS,), 0, CTX + 1)
    longest = jax.random.randint(place_key, (), 0, REQS)
    return jnp.where(jnp.arange(REQS) == longest, CTX, drawn).astype(jnp.int32)


def levels(own_key, shape, shards, least, top_value):
    factor_of, own = 1.0, jax.random.fold_in(own_key, 6)
    for axis_at, blocks in shards:
        draws = jnp.exp(jax.random.uniform(jax.random.fold_in(own, axis_at), (blocks,), jnp.float32, least / len(shards), top_value / len(shards)))
        factor_of = factor_of * jnp.repeat(draws, shape[axis_at] // blocks).reshape([-1 if axis == axis_at else 1 for axis in range(len(shape))])
    return factor_of


def routed_block(rng, own, number, rows, count, top, most, slope):
    sequence = jax.random.permutation(rng, count)
    crowded, usual = portions_of(count, rows * top, most, slope, True), portions_of(count, rows * top, most, slope, False)
    places = jnp.arange(count)

    def named(tallies, turn):
        used = int((tallies > 0).sum())
        fixed = max(1, used // 4)
        passed = fixed + (places - fixed + turn * (used - fixed)) % max(1, count - fixed)
        return jnp.zeros((count,), jnp.int32).at[sequence[jnp.where(places < fixed, places, passed)]].set(jnp.asarray(tallies, jnp.int32))

    tallies = jnp.where(number % 4 == 0, named(crowded, number // 4), named(usual, number - number // 4 - 1))
    mixed = jax.random.permutation(jax.random.fold_in(own, 3), count)
    donor, taker = mixed[0:count // 2 * 2:2], mixed[1:count // 2 * 2:2]
    slack = jnp.minimum(tallies[donor] - 1, most - tallies[taker]) // 2
    slack = jnp.where((donor == sequence[0]) | (taker == sequence[0]) | (tallies[taker] == 0), 0, jnp.maximum(slack, 0))
    passed = jax.random.randint(jax.random.fold_in(own, 4), (count // 2,), 0, 1 << 20) % (slack + 1)
    tallies = tallies.at[donor].add(-passed).at[taker].add(passed)
    members = jnp.searchsorted(jnp.cumsum(tallies), jnp.arange(rows * top), side="right").astype(jnp.int32)
    listing = members.reshape(top, rows).T
    listing = listing[jax.random.permutation(jax.random.fold_in(own, 1), rows)]
    turn = jax.random.randint(jax.random.fold_in(own, 2), (rows, 1), 0, top)
    return jnp.take_along_axis(listing, (jnp.arange(top)[None, :] + turn) % top, axis=1)


def portions_of(number_of, total, limit, slope, full):
    portions = [(1 << 20) // math.isqrt(standing ** slope) + 1 for standing in range(1, number_of + 1)]
    largest = limit if full else min(limit, max(-(-total // number_of), total * portions[0] // sum(portions)))
    least = 1 if total - largest >= number_of - 1 else 0
    counts, surplus = [largest] + [least] * (number_of - 1), total - largest - least * (number_of - 1)
    while surplus > 0:
        candidates = [i for i in range(1, number_of) if counts[i] < largest] or [i for i in range(1, number_of) if counts[i] < limit]
        mass, remaining = sum([portions[i] for i in candidates]), surplus
        for i in candidates:
            addition = min(limit - counts[i], max(1, remaining * portions[i] // mass), surplus)
            counts[i] = counts[i] + addition
            surplus = surplus - addition
    return np.array(counts)


def gaussian(own_key, shape, spread, reach, split=(), kind=jnp.bfloat16):
    values = jax.random.normal(own_key, shape, jnp.float32) * spread
    if len(split) > 0:
        values = levels(own_key, shape, split, -0.22, 0.18) * values
    return jnp.clip(values, min=-reach, max=reach).astype(kind)


def setup_inputs(seed: int = 0) -> dict:
    splits = jax.random.split(jax.random.key(seed), 14)
    tokens = gaussian(splits[0], (REQS, NEW_TOK, D), 1.0, 6.0, ((0, 8),))
    attn_gain = jnp.clip(1.0 + 0.18 * jax.random.normal(splits[1], (D,), jnp.float32), 0.1, 1.9)
    w_qkv = gaussian(splits[2], (D, KVH * (GROUP + 2) * HD), D ** -0.5, 0.109375, ((1, 4),))
    sink_logits = jnp.clip(10.0 * jax.random.uniform(splits[3], (QH,), jnp.float32) ** levels(splits[3], (QH,), ((0, 4),), -0.2, 0.2), 0.0, 10.0)
    w_out = gaussian(splits[4], (QH * HD, D), (QH * HD) ** -0.5, 0.09375, ((0, 4),))
    kv_cache = draw_kv_cache(jax.random.fold_in(splits[13], 71), 0)
    page_table = jax.vmap(lambda own: jax.random.permutation(own, PAGES_DEV))(jax.random.split(splits[6], REQS)).reshape((REQS, PAGES_DEV)).astype(jnp.int32)
    cache_lengths = draw_cache_lengths(jax.random.fold_in(splits[13], 71), 0)
    moe_gain = jnp.clip(1.0 + 0.18 * jax.random.normal(splits[8], (D,), jnp.float32), 0.1, 1.9)
    routes_keys = jax.random.split(jax.random.fold_in(splits[9], 1), REQS * NEW_TOK // ROWS_DEV)
    routes_turns = jax.random.permutation(jax.random.fold_in(splits[9], 3), REQS * NEW_TOK // ROWS_DEV)
    routes = jax.vmap(lambda own, number: routed_block(jax.random.fold_in(splits[9], 2), own, number, ROWS_DEV, EXPERTS, TOP, CAP, 1))(routes_keys, routes_turns).reshape((REQS, NEW_TOK, TOP))
    gate_weights = jnp.clip(0.1 + 0.59999999 * jax.random.uniform(splits[10], (REQS, NEW_TOK, TOP), jnp.float32) ** levels(splits[10], (REQS, NEW_TOK, TOP), ((0, 8),), -0.2, 0.2), 0.1, 0.7)
    w_gate_up = gaussian(splits[11], (EXPERTS, 2, D, FF), D ** -0.5, 0.109375, ((0, 8), (3, 4)))
    w_down = gaussian(splits[12], (EXPERTS, FF, D), FF ** -0.5, 0.109375, ((0, 8), (1, 4)))
    return {"tokens": tokens, "attn_gain": attn_gain, "w_qkv": w_qkv, "sink_logits": sink_logits, "w_out": w_out, "kv_cache": kv_cache, "page_table": page_table, "cache_lengths": cache_lengths, "moe_gain": moe_gain, "routes": routes, "gate_weights": gate_weights, "w_gate_up": w_gate_up, "w_down": w_down}


THETA_BASE = 150000.0
EPSILON = 1e-05
ALPHA_GLU = 1.702

def rms_scale(row_data, gain_vector):
    row_data = row_data.astype(jnp.float32)
    mean_square = lax.optimization_barrier(jnp.mean(row_data * row_data, axis=-1, keepdims=True))
    return row_data * lax.rsqrt(mean_square + EPSILON) * gain_vector

def rotate(vectors, positions):
    half_dim = vectors.shape[-1] // 2
    frequency = THETA_BASE ** (-(jnp.arange(half_dim, dtype=jnp.float32) * 2.0 / vectors.shape[-1]))
    angles = positions.astype(jnp.float32)[:, None] * frequency[None, :]
    view_shape = (vectors.shape[0],) + (1,) * (vectors.ndim - 2) + (half_dim,)
    cosine = jnp.cos(angles).reshape(view_shape)
    sine_part = jnp.sin(angles).reshape(view_shape)
    first_half = vectors[..., :half_dim]
    second_half = vectors[..., half_dim:]
    return jnp.concatenate([first_half * cosine - second_half * sine_part, second_half * cosine + first_half * sine_part], axis=-1)

def request_attention(tokens, kv_pages, cached_length, attn_gain, w_qkv, sink_logits, w_out):
    normed = rms_scale(tokens, attn_gain).astype(jnp.bfloat16)
    projected = jnp.dot(normed, w_qkv, preferred_element_type=jnp.float32).reshape(NEW_TOK, KVH, GROUP + 2, HD)
    positions = cached_length + jnp.arange(NEW_TOK, dtype=jnp.int32)
    queries = rotate(projected[:, :, :GROUP], positions).astype(jnp.bfloat16)
    new_keys = rotate(projected[:, :, GROUP], positions).astype(jnp.bfloat16)
    new_values = projected[:, :, GROUP + 1].astype(jnp.bfloat16)
    cached = kv_pages.reshape(CTX, KVH, 2, HD)
    all_keys = jnp.concatenate([cached[:, :, 0], new_keys], axis=0)
    all_values = jnp.concatenate([cached[:, :, 1], new_values], axis=0)
    key_position = jnp.arange(CTX + NEW_TOK, dtype=jnp.int32)
    query_position = jnp.arange(NEW_TOK, dtype=jnp.int32)
    visible = jnp.where(key_position[None, :] < CTX, key_position[None, :] < cached_length, key_position[None, :] - CTX <= query_position[:, None])
    score_scale = HD ** (-0.5)

    def head_attention(operands):
        query_head, key_head, value_head, sink_head = operands
        scores = jnp.einsum('qgd,kd->gqk', query_head.astype(jnp.float32), key_head.astype(jnp.float32)) * score_scale
        masked = jnp.where(visible[None], scores, -jnp.inf)
        peak = jnp.maximum(lax.optimization_barrier(jnp.max(masked, axis=-1)), sink_head[:, None])
        weights = jnp.where(visible[None], jnp.exp(scores - peak[..., None]), 0.0)
        denominator = lax.optimization_barrier(jnp.sum(weights, axis=-1)) + jnp.exp(sink_head[:, None] - peak)
        probs = weights.astype(jnp.bfloat16)
        numerator = jnp.einsum('gqk,kd->gqd', probs.astype(jnp.float32), value_head.astype(jnp.float32))
        return (numerator / denominator[..., None]).astype(jnp.bfloat16)
    attended = lax.map(head_attention, (queries.transpose(1, 0, 2, 3), all_keys.transpose(1, 0, 2), all_values.transpose(1, 0, 2), sink_logits.reshape(KVH, GROUP)))
    attended = attended.transpose(2, 0, 1, 3).reshape(NEW_TOK, QH * HD)
    return tokens.astype(jnp.float32) + jnp.dot(attended, w_out, preferred_element_type=jnp.float32)

def reference(tokens, attn_gain, w_qkv, sink_logits, w_out, kv_cache, page_table, cache_lengths, moe_gain, routes, gate_weights, w_gate_up, w_down):

    def per_request(request):
        kv_pages = kv_cache[request * PAGES_DEV + page_table[request]]
        return request_attention(tokens[request], kv_pages, cache_lengths[request], attn_gain, w_qkv, sink_logits, w_out)
    residual = lax.map(per_request, jnp.arange(REQS, dtype=jnp.int32)).reshape(REQS * NEW_TOK, D)
    moe_in = rms_scale(residual, moe_gain).astype(jnp.bfloat16)
    route_flat = routes.reshape(REQS * NEW_TOK, TOP)
    gate_flat = gate_weights.reshape(REQS * NEW_TOK, TOP)
    most_rows = N_REQ * N_KV * CAP

    def expert_pass(moe_sum, operands):
        expert, gate_up, down_proj = operands
        route_hit = route_flat == expert
        token_weight = lax.optimization_barrier(jnp.sum(jnp.where(route_hit, gate_flat, 0.0), axis=1))
        chosen = jnp.any(route_hit, axis=1)
        row_count = jnp.sum(chosen.astype(jnp.int32))
        row_index = jnp.nonzero(chosen, size=most_rows, fill_value=0)[0].astype(jnp.int32)
        in_range = jnp.arange(most_rows, dtype=jnp.int32) < row_count
        selected = moe_in[row_index]
        gate_part = jnp.dot(selected, gate_up[0], preferred_element_type=jnp.float32)
        up_part = jnp.dot(selected, gate_up[1], preferred_element_type=jnp.float32)
        activated = (gate_part * jax.nn.sigmoid(ALPHA_GLU * gate_part) * (up_part + 1.0)).astype(jnp.bfloat16)
        expert_out = jnp.dot(activated, down_proj, preferred_element_type=jnp.float32)
        scaled = jnp.where(in_range, token_weight[row_index], 0.0)[:, None] * expert_out
        return (moe_sum.at[row_index].add(scaled), None)
    mixed, unused = lax.scan(expert_pass, jnp.zeros((REQS * NEW_TOK, D), jnp.float32), (jnp.arange(EXPERTS, dtype=jnp.int32), w_gate_up, w_down))
    return (residual + mixed).astype(jnp.bfloat16).reshape(REQS, NEW_TOK, D)
```

```python
import functools

import jax
import jax.numpy as jnp
from jax import lax
from jax.experimental import pallas as pl
from jax.experimental.pallas import tpu as pltpu
from jax.sharding import PartitionSpec as P

HD = 64
TOP = 4
GROUP = 8


THETA_BASE = 150000.0
EPSILON = 1e-05
ALPHA_GLU = 1.702


def rms_scale(row_data, gain_vector):
    row_data = row_data.astype(jnp.float32)
    mean_square = jnp.mean(row_data * row_data, axis=-1, keepdims=True)
    return row_data * lax.rsqrt(mean_square + EPSILON) * gain_vector


LANES = 2 * HD
PAGE_STEP = 8
FINITE = 1e37


def attend_kernel(
    pages_ref,
    length_ref,
    token_ref,
    gain_ref,
    trig_ref,
    sink_ref,
    qkv_hbm,
    out_hbm,
    cache_hbm,
    partial_ref,
    qkv_ref,
    weight_ref,
    cache_ref,
    query_ref,
    total_ref,
    peak_ref,
    attended_ref,
    qkv_sem,
    weight_sem,
    cache_sem,
):
    heads, _, columns = query_ref.shape
    new_count = token_ref.shape[0]
    page_size = cache_hbm.shape[1]
    span = PAGE_STEP * page_size
    head_width = (GROUP + 2) * HD
    length = length_ref[0]
    chunks = (length + span - 1) // span
    whole_chunks = length // span

    def qkv_copy(head):
        part = slice(head * head_width, (head + 1) * head_width)
        return pltpu.make_async_copy(
            qkv_hbm.at[:, part], qkv_ref.at[:, part], qkv_sem.at[head]
        )

    weight_copy = pltpu.make_async_copy(out_hbm, weight_ref, weight_sem)
    for head in range(heads):
        qkv_copy(head).start()

    def fetch(chunk, _):
        for place in range(PAGE_STEP):
            at = chunk * PAGE_STEP + place
            pltpu.make_async_copy(
                cache_hbm.at[pages_ref[at]],
                cache_ref.at[pl.ds(pl.multiple_of(at * page_size, page_size), page_size)],
                cache_sem.at[chunk],
            ).start()
        return 0

    lax.fori_loop(0, chunks, fetch, 0)
    weight_copy.start()

    def key_side(block):
        lane = lax.broadcasted_iota(jnp.int32, block.shape, 1)
        return jnp.where(lane < HD, block, jnp.ones_like(block))

    def value_side(block):
        lane = lax.broadcasted_iota(jnp.int32, block.shape, 1)
        return jnp.where(lane < HD, jnp.ones_like(block), block)

    def weighted(block, weights):
        return lax.dot_general(
            block, weights, (((0,), (0,)), ((), ())), preferred_element_type=jnp.float32
        )

    normed = rms_scale(token_ref[...], gain_ref[...]).astype(jnp.bfloat16)
    cosine = trig_ref[:, :LANES]
    sine = trig_ref[:, LANES:]
    lane = lax.broadcasted_iota(jnp.int32, (new_count, LANES), 1)

    def turned(block):
        swapped = jnp.where(
            lane % HD < HD // 2,
            pltpu.roll(block, LANES - HD // 2, 1),
            pltpu.roll(block, HD // 2, 1),
        )
        return block * cosine + swapped * sine

    key_at = lax.broadcasted_iota(jnp.int32, (new_count, columns), 0)
    query_at = lax.broadcasted_iota(jnp.int32, (new_count, columns), 1) % new_count
    causal = key_at <= query_at
    row = lax.broadcasted_iota(jnp.int32, (LANES, columns), 0)
    fresh_blocks = []
    for head in range(heads):
        qkv_copy(head).wait()
        projected = jnp.dot(
            normed,
            qkv_ref[:, head * head_width : (head + 1) * head_width],
            preferred_element_type=jnp.float32,
        )
        for pair in range(GROUP // 2):
            block = turned(projected[:, pair * LANES : (pair + 1) * LANES])
            block = (block * (HD**-0.5)).T.astype(jnp.bfloat16)
            for half in range(2):
                at = (2 * pair + half) * new_count
                query_ref[head, :HD, at : at + new_count] = block[half * HD : (half + 1) * HD]
        query_ref[head, HD:, :] = jnp.zeros((HD, columns), jnp.bfloat16)
        block = projected[:, GROUP * HD :]
        fresh_blocks.append(jnp.where(lane < HD, turned(block), block).astype(jnp.bfloat16))

    def begin(head):
        block = fresh_blocks[head]
        scores = jnp.dot(block, query_ref[head], preferred_element_type=jnp.float32)
        scores = jnp.where(causal, scores, -jnp.inf)
        sink = sink_ref[head : head + 1, :]
        peak = jnp.maximum(sink, jnp.max(scores, axis=0, keepdims=True))
        weights = jnp.exp(scores - peak).astype(jnp.bfloat16)
        start = jnp.where(row < HD, jnp.exp(sink - peak), 0.0)
        total_ref[head] = start + weighted(value_side(block), weights)
        peak_ref[head : head + 1, :] = peak

    for head in range(heads):
        begin(head)
        peak = -peak_ref[head : head + 1, :]
        first = peak.astype(jnp.bfloat16).astype(jnp.float32)
        second = (peak - first).astype(jnp.bfloat16).astype(jnp.float32)
        third = peak - first - second
        tail_row = lax.broadcasted_iota(jnp.int32, (HD, columns), 0)
        shift = jnp.where(
            tail_row == 0,
            first,
            jnp.where(tail_row == 1, second, jnp.where(tail_row == 2, third, 0.0)),
        )
        query_ref[head, HD:, :] = shift.astype(jnp.bfloat16)

    def chunk_at(chunk):
        return pl.ds(pl.multiple_of(chunk * span, span), span)

    def absorb(chunk, masked):
        keys = cache_ref.at[chunk_at(chunk)]
        pltpu.make_async_copy(keys, keys, cache_sem.at[chunk]).wait()
        for head in range(heads):
            block = cache_ref[chunk_at(chunk), head * LANES : (head + 1) * LANES]
            scores = jnp.dot(
                key_side(block), query_ref[head], preferred_element_type=jnp.float32
            )
            weights = jnp.exp(scores)
            if masked:
                at = chunk * span + lax.broadcasted_iota(jnp.int32, scores.shape, 0)
                weights = jnp.where(at < length, weights, 0.0)
            total_ref[head] += weighted(value_side(block), weights.astype(jnp.bfloat16))

    def absorb_whole(chunk, _):
        absorb(chunk, False)
        return 0

    lax.fori_loop(0, whole_chunks, absorb_whole, 0)

    @pl.when(chunks > whole_chunks)
    def _():
        absorb(whole_chunks, True)

    largest = jnp.max(jnp.where(jnp.abs(total_ref[...]) < FINITE, 0.0, 1.0))

    @pl.when(largest > 0.5)
    def _():
        for head in range(heads):
            query_ref[head, HD:, :] = jnp.zeros((HD, columns), jnp.bfloat16)
        for head in range(heads):
            begin(head)

        def again(chunk, _):
            for head in range(heads):
                block = cache_ref[chunk_at(chunk), head * LANES : (head + 1) * LANES]
                scores = jnp.dot(block, query_ref[head], preferred_element_type=jnp.float32)
                at = chunk * span + lax.broadcasted_iota(jnp.int32, scores.shape, 0)
                scores = jnp.where(at < length, scores, -jnp.inf)
                old_peak = peak_ref[head : head + 1, :]
                peak = jnp.maximum(old_peak, jnp.max(scores, axis=0, keepdims=True))
                weights = jnp.exp(scores - peak).astype(jnp.bfloat16)
                total_ref[head] = total_ref[head] * jnp.exp(old_peak - peak) + weighted(
                    value_side(block), weights
                )
                peak_ref[head : head + 1, :] = peak
            return 0

        lax.fori_loop(0, chunks, again, 0)

    for head in range(heads):
        for pair in range(GROUP // 2):
            parts = []
            for half in range(2):
                at = (2 * pair + half) * new_count
                part = total_ref[head, :, at : at + new_count]
                parts.append(part[HD:] / part[0:1])
            block = jnp.concatenate(parts, axis=0).T.astype(jnp.bfloat16)
            at = head * GROUP * HD + pair * LANES
            attended_ref[:, at : at + LANES] = block
    weight_copy.wait()
    partial_ref[...] = jnp.dot(
        attended_ref[...], weight_ref[...], preferred_element_type=jnp.float32
    ).astype(jnp.bfloat16)


def attend(tokens, attn_gain, w_qkv, sink_rows, w_out, kv_cache, page_row, cached_length):
    new_count, width = tokens.shape
    heads = sink_rows.shape[0]
    columns = GROUP * new_count
    pages, page_size, cache_width = kv_cache.shape
    half = HD // 2
    frequency = THETA_BASE ** (-(jnp.arange(half, dtype=jnp.float32) * 2.0 / HD))
    positions = cached_length[0] + jnp.arange(new_count, dtype=jnp.int32)
    angles = positions.astype(jnp.float32)[:, None] * frequency[None, :]
    cosine = jnp.cos(angles)
    sine = jnp.sin(angles)
    trig = jnp.concatenate([cosine] * 4 + [-sine, sine, -sine, sine], axis=1)
    sinks = jnp.repeat(sink_rows, new_count, axis=1)
    scalars = pl.BlockSpec(memory_space=pltpu.SMEM)
    dense = pl.BlockSpec(memory_space=pltpu.VMEM)
    apart = pl.BlockSpec(memory_space=pl.ANY)
    return pl.pallas_call(
        attend_kernel,
        in_specs=[scalars, scalars, dense, dense, dense, dense, apart, apart, apart],
        out_specs=dense,
        out_shape=jax.ShapeDtypeStruct((new_count, width), jnp.bfloat16),
        scratch_shapes=[
            pltpu.VMEM(w_qkv.shape, jnp.bfloat16),
            pltpu.VMEM(w_out.shape, jnp.bfloat16),
            pltpu.VMEM((pages * page_size, cache_width), jnp.bfloat16),
            pltpu.VMEM((heads, LANES, columns), jnp.bfloat16),
            pltpu.VMEM((heads, LANES, columns), jnp.float32),
            pltpu.VMEM((heads, columns), jnp.float32),
            pltpu.VMEM((new_count, heads * GROUP * HD), jnp.bfloat16),
            pltpu.SemaphoreType.DMA((heads,)),
            pltpu.SemaphoreType.DMA,
            pltpu.SemaphoreType.DMA((pages // PAGE_STEP,)),
        ],
        compiler_params=pltpu.CompilerParams(vmem_limit_bytes=56 * 1024 * 1024),
        name="attend",
    )(page_row, cached_length, tokens, attn_gain[None], trig, sinks, w_qkv, w_out, kv_cache)


def on_device(
    tokens,
    attn_gain,
    w_qkv,
    sink_logits,
    w_out,
    kv_cache,
    page_table,
    cache_lengths,
    moe_gain,
    routes,
    gate_weights,
    w_gate_up,
    w_down,
):
    kv_count = lax.axis_size("kv")
    req_count = lax.axis_size("req")
    place = lax.axis_index("kv")
    new_count = tokens.shape[1]
    rows_dev = new_count // kv_count
    heads_dev = w_qkv.shape[1] // ((GROUP + 2) * HD)
    own_tokens = tokens[0]
    experts_dev = w_gate_up.shape[0]
    experts_all = experts_dev * req_count
    hidden_dev = w_down.shape[1]

    chosen = routes[0][:, :, None] == jnp.arange(experts_all, dtype=jnp.int32)
    expert_gates = jnp.sum(jnp.where(chosen, gate_weights[0][:, :, None], 0.0), axis=1)
    own_part = lax.dynamic_slice_in_dim(expert_gates, place * rows_dev, rows_dev, 0)
    all_gates = lax.all_gather(own_part, ("req", "kv"), axis=0, tiled=True)
    own_gates = lax.dynamic_slice_in_dim(
        all_gates, lax.axis_index("req") * experts_dev, experts_dev, 1
    )

    partial_out = attend(
        own_tokens,
        attn_gain,
        w_qkv,
        sink_logits.reshape(heads_dev, GROUP),
        w_out,
        kv_cache,
        page_table[0],
        cache_lengths,
    )
    summed_out = lax.psum_scatter(
        partial_out, "kv", scatter_dimension=0, tiled=True
    ).astype(jnp.float32)
    own_rows = lax.dynamic_slice_in_dim(own_tokens, place * rows_dev, rows_dev, 0)
    residual = own_rows.astype(jnp.float32) + summed_out
    moe_rows = rms_scale(residual, moe_gain).astype(jnp.bfloat16)
    moe_in = lax.all_gather(moe_rows, ("req", "kv"), axis=0, tiled=True)
    hidden = []
    for expert in range(experts_dev):
        gate_part = jnp.dot(moe_in, w_gate_up[expert, 0], preferred_element_type=jnp.float32)
        up_part = jnp.dot(moe_in, w_gate_up[expert, 1], preferred_element_type=jnp.float32)
        activated = gate_part * jax.nn.sigmoid(ALPHA_GLU * gate_part) * (up_part + 1.0)
        hidden.append((activated * own_gates[:, expert : expert + 1]).astype(jnp.bfloat16))
    mixed_part = jnp.dot(
        jnp.concatenate(hidden, axis=1),
        w_down.reshape(experts_dev * hidden_dev, -1),
        preferred_element_type=jnp.float32,
    ).astype(jnp.bfloat16)
    mixture = lax.psum_scatter(
        mixed_part, ("req", "kv"), scatter_dimension=0, tiled=True
    ).astype(jnp.float32)
    return (residual + mixture).astype(jnp.bfloat16)[None]


def solution(mesh):
    in_specs = (
        P("req", None, None),
        P(),
        P(None, "kv"),
        P("kv"),
        P("kv", None),
        P("req", None, "kv"),
        P("req", None),
        P("req"),
        P(),
        P("req", None, None),
        P("req", None, None),
        P("req", None, None, "kv"),
        P("req", "kv", None),
    )
    out_specs = P("req", "kv", None)
    return jax.shard_map(
        on_device, mesh=mesh, in_specs=in_specs, out_specs=out_specs, check_vma=False
    )
```

```python
import functools

import jax
import jax.numpy as jnp
from jax import lax
from jax.experimental import pallas as pl
from jax.experimental.pallas import tpu as pltpu
from jax.sharding import PartitionSpec as P

HD = 64
TOP = 4
GROUP = 8


THETA_BASE = 150000.0
EPSILON = 1e-05
ALPHA_GLU = 1.702


def rms_scale(row_data, gain_vector):
    row_data = row_data.astype(jnp.float32)
    mean_square = jnp.mean(row_data * row_data, axis=-1, keepdims=True)
    return row_data * lax.rsqrt(mean_square + EPSILON) * gain_vector


LANES = 2 * HD
PAGE_STEP = 8
FINITE = 1e37


def attend_kernel(
    pages_ref,
    length_ref,
    token_ref,
    gain_ref,
    trig_ref,
    sink_ref,
    qkv_hbm,
    out_hbm,
    cache_hbm,
    partial_ref,
    qkv_ref,
    weight_ref,
    cache_ref,
    query_ref,
    total_ref,
    peak_ref,
    attended_ref,
    qkv_sem,
    weight_sem,
    cache_sem,
):
    heads, _, columns = query_ref.shape
    new_count = token_ref.shape[0]
    page_size = cache_hbm.shape[1]
    span = PAGE_STEP * page_size
    head_width = (GROUP + 2) * HD
    length = length_ref[0]
    chunks = (length + span - 1) // span
    whole_chunks = length // span

    def qkv_copy(head):
        part = slice(head * head_width, (head + 1) * head_width)
        return pltpu.make_async_copy(
            qkv_hbm.at[:, part], qkv_ref.at[:, part], qkv_sem.at[head]
        )

    weight_copy = pltpu.make_async_copy(out_hbm, weight_ref, weight_sem)
    for head in range(heads):
        qkv_copy(head).start()

    def fetch(chunk, _):
        for place in range(PAGE_STEP):
            at = chunk * PAGE_STEP + place
            pltpu.make_async_copy(
                cache_hbm.at[pages_ref[at]],
                cache_ref.at[pl.ds(pl.multiple_of(at * page_size, page_size), page_size)],
                cache_sem.at[chunk],
            ).start()
        return 0

    lax.fori_loop(0, chunks, fetch, 0)
    weight_copy.start()

    def key_side(block):
        lane = lax.broadcasted_iota(jnp.int32, block.shape, 1)
        return jnp.where(lane < HD, block, jnp.ones_like(block))

    def value_side(block):
        lane = lax.broadcasted_iota(jnp.int32, block.shape, 1)
        return jnp.where(lane < HD, jnp.ones_like(block), block)

    def weighted(block, weights):
        return lax.dot_general(
            block, weights, (((0,), (0,)), ((), ())), preferred_element_type=jnp.float32
        )

    normed = rms_scale(token_ref[...], gain_ref[...]).astype(jnp.bfloat16)
    cosine = trig_ref[:, :LANES]
    sine = trig_ref[:, LANES:]
    lane = lax.broadcasted_iota(jnp.int32, (new_count, LANES), 1)

    def turned(block):
        swapped = jnp.where(
            lane % HD < HD // 2,
            pltpu.roll(block, LANES - HD // 2, 1),
            pltpu.roll(block, HD // 2, 1),
        )
        return block * cosine + swapped * sine

    key_at = lax.broadcasted_iota(jnp.int32, (new_count, columns), 0)
    query_at = lax.broadcasted_iota(jnp.int32, (new_count, columns), 1) % new_count
    causal = key_at <= query_at
    row = lax.broadcasted_iota(jnp.int32, (LANES, columns), 0)
    fresh_blocks = []
    for head in range(heads):
        qkv_copy(head).wait()
        projected = jnp.dot(
            normed,
            qkv_ref[:, head * head_width : (head + 1) * head_width],
            preferred_element_type=jnp.float32,
        )
        for pair in range(GROUP // 2):
            block = turned(projected[:, pair * LANES : (pair + 1) * LANES])
            block = (block * (HD**-0.5)).T.astype(jnp.bfloat16)
            for half in range(2):
                at = (2 * pair + half) * new_count
                query_ref[head, :HD, at : at + new_count] = block[half * HD : (half + 1) * HD]
        query_ref[head, HD:, :] = jnp.zeros((HD, columns), jnp.bfloat16)
        block = projected[:, GROUP * HD :]
        fresh_blocks.append(jnp.where(lane < HD, turned(block), block).astype(jnp.bfloat16))

    def begin(head):
        block = fresh_blocks[head]
        scores = jnp.dot(block, query_ref[head], preferred_element_type=jnp.float32)
        scores = jnp.where(causal, scores, -jnp.inf)
        sink = sink_ref[head : head + 1, :]
        peak = jnp.maximum(sink, jnp.max(scores, axis=0, keepdims=True))
        weights = jnp.exp(scores - peak).astype(jnp.bfloat16)
        start = jnp.where(row < HD, jnp.exp(sink - peak), 0.0)
        total_ref[head] = start + weighted(value_side(block), weights)
        peak_ref[head : head + 1, :] = peak

    for head in range(heads):
        begin(head)
        peak = -peak_ref[head : head + 1, :]
        first = peak.astype(jnp.bfloat16).astype(jnp.float32)
        second = (peak - first).astype(jnp.bfloat16).astype(jnp.float32)
        third = peak - first - second
        tail_row = lax.broadcasted_iota(jnp.int32, (HD, columns), 0)
        shift = jnp.where(
            tail_row == 0,
            first,
            jnp.where(tail_row == 1, second, jnp.where(tail_row == 2, third, 0.0)),
        )
        query_ref[head, HD:, :] = shift.astype(jnp.bfloat16)

    def chunk_at(chunk):
        return pl.ds(pl.multiple_of(chunk * span, span), span)

    def absorb(chunk, masked):
        keys = cache_ref.at[chunk_at(chunk)]
        pltpu.make_async_copy(keys, keys, cache_sem.at[chunk]).wait()
        for head in range(heads):
            block = cache_ref[chunk_at(chunk), head * LANES : (head + 1) * LANES]
            scores = jnp.dot(
                key_side(block), query_ref[head], preferred_element_type=jnp.float32
            )
            weights = jnp.exp(scores)
            if masked:
                at = chunk * span + lax.broadcasted_iota(jnp.int32, scores.shape, 0)
                weights = jnp.where(at < length, weights, 0.0)
            total_ref[head] += weighted(value_side(block), weights.astype(jnp.bfloat16))

    def absorb_whole(chunk, _):
        absorb(chunk, False)
        return 0

    lax.fori_loop(0, whole_chunks, absorb_whole, 0)

    @pl.when(chunks > whole_chunks)
    def _():
        absorb(whole_chunks, True)

    largest = jnp.max(jnp.where(jnp.abs(total_ref[...]) < FINITE, 0.0, 1.0))

    @pl.when(largest > 0.5)
    def _():
        for head in range(heads):
            query_ref[head, HD:, :] = jnp.zeros((HD, columns), jnp.bfloat16)
        for head in range(heads):
            begin(head)

        def again(chunk, _):
            for head in range(heads):
                block = cache_ref[chunk_at(chunk), head * LANES : (head + 1) * LANES]
                scores = jnp.dot(block, query_ref[head], preferred_element_type=jnp.float32)
                at = chunk * span + lax.broadcasted_iota(jnp.int32, scores.shape, 0)
                scores = jnp.where(at < length, scores, -jnp.inf)
                old_peak = peak_ref[head : head + 1, :]
                peak = jnp.maximum(old_peak, jnp.max(scores, axis=0, keepdims=True))
                weights = jnp.exp(scores - peak).astype(jnp.bfloat16)
                total_ref[head] = total_ref[head] * jnp.exp(old_peak - peak) + weighted(
                    value_side(block), weights
                )
                peak_ref[head : head + 1, :] = peak
            return 0

        lax.fori_loop(0, chunks, again, 0)

    for head in range(heads):
        for pair in range(GROUP // 2):
            parts = []
            for half in range(2):
                at = (2 * pair + half) * new_count
                part = total_ref[head, :, at : at + new_count]
                parts.append(part[HD:] / part[0:1])
            block = jnp.concatenate(parts, axis=0).T.astype(jnp.bfloat16)
            at = head * GROUP * HD + pair * LANES
            attended_ref[:, at : at + LANES] = block
    weight_copy.wait()
    partial_ref[...] = lax.dot_general(
        attended_ref[...],
        weight_ref[...],
        (((1,), (1,)), ((), ())),
        preferred_element_type=jnp.float32,
    ).astype(jnp.bfloat16)


def attend(tokens, attn_gain, w_qkv, sink_rows, w_out, kv_cache, page_row, cached_length):
    new_count, width = tokens.shape
    heads = sink_rows.shape[0]
    columns = GROUP * new_count
    pages, page_size, cache_width = kv_cache.shape
    half = HD // 2
    frequency = THETA_BASE ** (-(jnp.arange(half, dtype=jnp.float32) * 2.0 / HD))
    positions = cached_length[0] + jnp.arange(new_count, dtype=jnp.int32)
    angles = positions.astype(jnp.float32)[:, None] * frequency[None, :]
    cosine = jnp.cos(angles)
    sine = jnp.sin(angles)
    trig = jnp.concatenate([cosine] * 4 + [-sine, sine, -sine, sine], axis=1)
    sinks = jnp.repeat(sink_rows, new_count, axis=1)
    scalars = pl.BlockSpec(memory_space=pltpu.SMEM)
    dense = pl.BlockSpec(memory_space=pltpu.VMEM)
    apart = pl.BlockSpec(memory_space=pl.ANY)
    return pl.pallas_call(
        attend_kernel,
        in_specs=[scalars, scalars, dense, dense, dense, dense, apart, apart, apart],
        out_specs=dense,
        out_shape=jax.ShapeDtypeStruct((new_count, width), jnp.bfloat16),
        scratch_shapes=[
            pltpu.VMEM(w_qkv.shape, jnp.bfloat16),
            pltpu.VMEM(w_out.shape[::-1], jnp.bfloat16),
            pltpu.VMEM((pages * page_size, cache_width), jnp.bfloat16),
            pltpu.VMEM((heads, LANES, columns), jnp.bfloat16),
            pltpu.VMEM((heads, LANES, columns), jnp.float32),
            pltpu.VMEM((heads, columns), jnp.float32),
            pltpu.VMEM((new_count, heads * GROUP * HD), jnp.bfloat16),
            pltpu.SemaphoreType.DMA((heads,)),
            pltpu.SemaphoreType.DMA,
            pltpu.SemaphoreType.DMA((pages // PAGE_STEP,)),
        ],
        compiler_params=pltpu.CompilerParams(vmem_limit_bytes=56 * 1024 * 1024),
        name="attend",
    )(page_row, cached_length, tokens, attn_gain[None], trig, sinks, w_qkv, w_out.T, kv_cache)


def moe_kernel(
    partial_ref,
    token_ref,
    gain_ref,
    gate_ref,
    up_hbm,
    down_hbm,
    out_ref,
    up_ref,
    down_ref,
    gathered_ref,
    mixed_ref,
    mate_ref,
    plane_ref,
    column_ref,
    share_ref,
    total_ref,
    residual_ref,
    up_sem,
    down_sem,
    share_sem,
    gather_sem,
    gather_mate_sem,
    mate_sem,
    plane_sem,
    column_sem,
    sent_sem,
    *,
    grid_z,
    grid_y,
    grid_x,
):
    req, kv = lax.axis_index("req"), lax.axis_index("kv")
    kv_count = 2 * grid_x
    z, y = req // grid_y, req % grid_y
    x, core = kv // 2, kv % 2
    blocks, rows, width = mixed_ref.shape
    last_tile = width // 128 * 128
    experts = up_hbm.shape[0]
    plane_blocks = grid_y * kv_count
    xs, ys = range(1, grid_x), range(1, grid_y)

    def at_kv(other):
        return (req, other)

    mate = at_kv(2 * x + 1 - core)

    def x_peer(step):
        return at_kv(2 * ((x + step) % grid_x) + core)

    def y_peer(step):
        return (z * grid_y + (y + step) % grid_y, kv)

    def z_peer(step):
        return (((z + step) % grid_z) * grid_y + y, kv)

    def origin(plane):
        return (z + grid_z - plane) % grid_z

    def block_at(plane, y_step, x_step, parity):
        row = origin(plane) * grid_y + (y + grid_y + y_step) % grid_y
        return row * kv_count + 2 * ((x + grid_x + x_step) % grid_x) + parity

    def remote(source, target, sent, received, device):
        return pltpu.make_async_remote_copy(
            src_ref=source,
            dst_ref=target,
            send_sem=sent,
            recv_sem=received,
            device_id=device,
            device_id_type=pl.DeviceIdType.MESH,
        )

    def arrived(block, received):
        pltpu.make_async_copy(block, block, received).wait()

    up_copies = [
        pltpu.make_async_copy(up_hbm.at[e], up_ref.at[e], up_sem.at[e]) for e in range(experts)
    ]
    down_copies = [
        pltpu.make_async_copy(down_hbm.at[e], down_ref.at[e], down_sem.at[e])
        for e in range(experts)
    ]
    for expert in range(experts):
        up_copies[expert].start()
        down_copies[expert].start()

    barrier = pltpu.get_barrier_semaphore()
    partners = [at_kv((kv + step) % kv_count) for step in range(1, kv_count)]
    partners += [y_peer(step) for step in ys] + [z_peer(step) for step in range(1, grid_z)]
    for device in partners:
        pl.semaphore_signal(
            barrier, inc=1, device_id=device, device_id_type=pl.DeviceIdType.MESH
        )
    pl.semaphore_wait(barrier, len(partners))

    def row_block(index):
        return pl.ds(pl.multiple_of(index * rows, rows), rows)

    for step in range(1, kv_count):
        other = (kv + step) % kv_count
        remote(
            partial_ref.at[row_block(other)],
            share_ref.at[step - 1],
            sent_sem.at[0],
            share_sem.at[step - 1],
            at_kv(other),
        ).start()
    summed = partial_ref[row_block(kv)].astype(jnp.float32)
    for step in range(1, kv_count):
        arrived(share_ref.at[step - 1], share_sem.at[step - 1])
        summed += share_ref[step - 1].astype(jnp.float32)
    residual = token_ref[row_block(kv)].astype(jnp.float32) + summed
    residual_ref[...] = residual
    own = block_at(0, 0, 0, core)
    gathered_ref[own, :, last_tile:] = gate_ref[row_block(kv)]
    gathered_ref[own, :, :width] = rms_scale(residual, gain_ref[...]).astype(jnp.bfloat16)

    def pass_on(block, received, device):
        remote(
            gathered_ref.at[block], gathered_ref.at[block], sent_sem.at[1], received, device
        ).start()

    for step in range(1, grid_z):
        pass_on(own, gather_sem.at[step, 0, 0], z_peer(step))

    def gather_own(plane):
        block = block_at(plane, 0, 0, core)

        @pl.when(plane > 0)
        def _():
            arrived(gathered_ref.at[block], gather_sem.at[plane, 0, 0])

        for j in xs:
            pass_on(block, gather_sem.at[plane, 0, j], x_peer(j))
        for i in ys:
            pass_on(block, gather_sem.at[plane, i, 0], y_peer(i))
        pass_on(block, gather_mate_sem.at[plane, 0, 0], mate)

    def gather_near(plane):
        def take(i, j):
            block = block_at(plane, -i, -j, core)
            arrived(gathered_ref.at[block], gather_sem.at[plane, i, j])
            return block

        @pl.when(plane % 2 == 0)
        def _():
            for i in ys:
                block = take(i, 0)
                for j in xs:
                    pass_on(block, gather_sem.at[plane, i, j], x_peer(j))
                pass_on(block, gather_mate_sem.at[plane, i, 0], mate)
            for j in xs:
                pass_on(take(0, j), gather_mate_sem.at[plane, 0, j], mate)

        @pl.when(plane % 2 == 1)
        def _():
            for j in xs:
                block = take(0, j)
                for i in ys:
                    pass_on(block, gather_sem.at[plane, i, j], y_peer(i))
                pass_on(block, gather_mate_sem.at[plane, 0, j], mate)
            for i in ys:
                pass_on(take(i, 0), gather_mate_sem.at[plane, i, 0], mate)

    def gather_far(plane):
        for i in ys:
            for j in xs:
                block = block_at(plane, -i, -j, core)
                arrived(gathered_ref.at[block], gather_sem.at[plane, i, j])
                pass_on(block, gather_mate_sem.at[plane, i, j], mate)

    def gather_last(plane):
        for i in range(grid_y):
            for j in range(grid_x):
                block = block_at(plane, -i, -j, 1 - core)
                arrived(gathered_ref.at[block], gather_mate_sem.at[plane, i, j])

    def compute(plane, expert):
        start = pl.multiple_of(origin(plane) * plane_blocks, plane_blocks)
        part = gathered_ref[pl.ds(start, plane_blocks), :, :width]
        part = part.reshape(plane_blocks * rows, width)

        def projected(which):
            return lax.dot_general(
                part,
                up_ref[expert, which],
                (((1,), (1,)), ((), ())),
                preferred_element_type=jnp.float32,
            )

        gate, up = projected(0), projected(1)
        gates = gathered_ref[pl.ds(start, plane_blocks), :, last_tile:].reshape(-1, 128)
        place = width - last_tile + req * experts + expert
        lane = lax.broadcasted_iota(jnp.int32, gates.shape, 1)
        choice = (lane == place) | (lane == place + experts * (blocks // kv_count))
        weight = jnp.sum(
            jnp.where(choice, gates.astype(jnp.float32), 0.0), axis=1, keepdims=True
        )
        hidden = gate * jax.nn.sigmoid(ALPHA_GLU * gate) * (up + 1.0) * weight
        mixed = jnp.dot(
            hidden.astype(jnp.bfloat16), down_ref[expert], preferred_element_type=jnp.float32
        )

        @pl.when(expert == 0)
        def _():
            total_ref[...] = mixed

        @pl.when(expert > 0)
        def _():
            total_ref[...] += mixed

        @pl.when(expert == experts - 1)
        def _():
            mixed_ref[pl.ds(start, plane_blocks)] = (
                total_ref[...].astype(jnp.bfloat16).reshape(plane_blocks, rows, width)
            )

    def hand_over(block, target, received, device):
        remote(mixed_ref.at[block], target, sent_sem.at[2], received, device).start()

    def add_to(block, terms):
        value = mixed_ref[block].astype(jnp.float32)
        for term in terms:
            value += term[...].astype(jnp.float32)
        mixed_ref[block] = value.astype(jnp.bfloat16)

    def sum_mate_send(plane):
        for i in range(grid_y):
            for j in range(grid_x):
                hand_over(
                    block_at(plane, i, j, 1 - core),
                    mate_ref.at[plane, i, j],
                    mate_sem.at[plane, i, j],
                    mate,
                )

    def plane_send(plane, i, j, device):
        hand_over(
            block_at(plane, i, j, core),
            plane_ref.at[plane, i, j],
            plane_sem.at[plane, i, j],
            device,
        )

    def plane_take(plane, i, j):
        arrived(plane_ref.at[plane, i, j], plane_sem.at[plane, i, j])
        return plane_ref.at[plane, i, j]

    def sum_mate(plane):
        for i in range(grid_y):
            for j in range(grid_x):
                arrived(mate_ref.at[plane, i, j], mate_sem.at[plane, i, j])
                add_to(block_at(plane, i, j, core), [mate_ref.at[plane, i, j]])

        @pl.when(plane % 2 == 0)
        def _():
            for j in xs:
                for i in list(ys) + [0]:
                    plane_send(plane, i, j, x_peer(j))

        @pl.when(plane % 2 == 1)
        def _():
            for i in ys:
                for j in list(xs) + [0]:
                    plane_send(plane, i, j, y_peer(i))

    def sum_near(plane):
        @pl.when(plane % 2 == 0)
        def _():
            for i in list(ys) + [0]:
                add_to(
                    block_at(plane, i, 0, core), [plane_take(plane, i, j) for j in xs]
                )
                if i:
                    plane_send(plane, i, 0, y_peer(i))

        @pl.when(plane % 2 == 1)
        def _():
            for j in list(xs) + [0]:
                add_to(
                    block_at(plane, 0, j, core), [plane_take(plane, i, j) for i in ys]
                )
                if j:
                    plane_send(plane, 0, j, x_peer(j))

    def sum_far(plane):
        block = block_at(plane, 0, 0, core)

        @pl.when(plane % 2 == 0)
        def _():
            add_to(block, [plane_take(plane, i, 0) for i in ys])

        @pl.when(plane % 2 == 1)
        def _():
            add_to(block, [plane_take(plane, 0, j) for j in xs])

        for step in range(1, grid_z):

            @pl.when(plane == step)
            def _():
                hand_over(
                    block,
                    column_ref.at[step - 1],
                    column_sem.at[step - 1],
                    z_peer(grid_z - step),
                )

    def run_at(step, first, task):
        shifted = step - first

        @pl.when((shifted >= 0) & (shifted < experts * grid_z) & (shifted % experts == 0))
        def _():
            task(shifted // experts)

    def advance(turn, _):
        step = turn
        run_at(step, 3 + experts, sum_mate_send)
        run_at(step, 2, gather_far)
        run_at(step, 1, gather_near)
        run_at(step, 0, gather_own)
        run_at(step, 4 + experts, sum_mate)
        run_at(step, 6 + experts, sum_near)
        run_at(step, 8 + experts, sum_far)
        run_at(step, 3, gather_last)
        at = step - 3
        for expert in range(experts):

            @pl.when(at == expert)
            def _():
                up_copies[expert].wait()
                down_copies[expert].wait()

        @pl.when((at >= 0) & (at < experts * grid_z))
        def _():
            compute(at // experts, at % experts)

        return 0

    lax.fori_loop(0, 9 + experts * grid_z, advance, 0)

    result = residual_ref[...] + mixed_ref[own].astype(jnp.float32)
    for step in range(1, grid_z):
        arrived(column_ref.at[step - 1], column_sem.at[step - 1])
        result += column_ref[step - 1].astype(jnp.float32)
    out_ref[...] = result.astype(jnp.bfloat16)
    arrived(share_ref, sent_sem.at[0])
    arrived(gathered_ref.at[: blocks - 1], sent_sem.at[1])
    arrived(mixed_ref.at[: blocks - 1], sent_sem.at[2])


def mixture(partial_out, tokens, moe_gain, expert_gates, w_gate_up, w_down):
    kv_count, req_count = lax.axis_size("kv"), lax.axis_size("req")
    new_count, width = tokens.shape
    rows = new_count // kv_count
    experts, hidden = w_down.shape[:2]
    blocks = kv_count * req_count
    grid_x = kv_count // 2
    grid_z = 4 if req_count % 4 == 0 else req_count
    grid_y = req_count // grid_z
    dense = pl.BlockSpec(memory_space=pltpu.VMEM)
    apart = pl.BlockSpec(memory_space=pl.ANY)
    half = jnp.bfloat16
    lead = width % 128
    upper = expert_gates.astype(half)
    lower = (expert_gates - upper.astype(jnp.float32)).astype(half)
    gate_tail = jnp.pad(jnp.concatenate([upper, lower], axis=1), ((0, 0), (lead, 0)))
    gate_tail = jnp.pad(gate_tail, ((0, 0), (0, -gate_tail.shape[1] % 128)))
    full_width = width - lead + gate_tail.shape[1]
    return pl.pallas_call(
        functools.partial(moe_kernel, grid_z=grid_z, grid_y=grid_y, grid_x=grid_x),
        in_specs=[dense, dense, dense, dense, apart, apart],
        out_specs=dense,
        out_shape=jax.ShapeDtypeStruct((rows, width), half),
        scratch_shapes=[
            pltpu.VMEM((experts, 2, hidden, width), half),
            pltpu.VMEM(w_down.shape, half),
            pltpu.VMEM((blocks, rows, full_width), half),
            pltpu.VMEM((blocks, rows, width), half),
            pltpu.VMEM((grid_z, grid_y, grid_x, rows, width), half),
            pltpu.VMEM((grid_z, grid_y, grid_x, rows, width), half),
            pltpu.VMEM((grid_z - 1, rows, width), half),
            pltpu.VMEM((kv_count - 1, rows, width), half),
            pltpu.VMEM((blocks // grid_z * rows, width), jnp.float32),
            pltpu.VMEM((rows, width), jnp.float32),
            pltpu.SemaphoreType.DMA((experts,)),
            pltpu.SemaphoreType.DMA((experts,)),
            pltpu.SemaphoreType.DMA((kv_count - 1,)),
            pltpu.SemaphoreType.DMA((grid_z, grid_y, grid_x)),
            pltpu.SemaphoreType.DMA((grid_z, grid_y, grid_x)),
            pltpu.SemaphoreType.DMA((grid_z, grid_y, grid_x)),
            pltpu.SemaphoreType.DMA((grid_z, grid_y, grid_x)),
            pltpu.SemaphoreType.DMA((grid_z - 1,)),
            pltpu.SemaphoreType.DMA((3,)),
        ],
        compiler_params=pltpu.CompilerParams(
            vmem_limit_bytes=63 * 1024 * 1024, collective_id=0, has_side_effects=True
        ),
        name="mixture",
    )(partial_out, tokens, moe_gain[None], gate_tail, jnp.swapaxes(w_gate_up, 2, 3), w_down)


def on_device(
    tokens,
    attn_gain,
    w_qkv,
    sink_logits,
    w_out,
    kv_cache,
    page_table,
    cache_lengths,
    moe_gain,
    routes,
    gate_weights,
    w_gate_up,
    w_down,
):
    heads_dev = w_qkv.shape[1] // ((GROUP + 2) * HD)
    own_tokens = tokens[0]
    experts_dev = w_gate_up.shape[0]
    experts_all = experts_dev * lax.axis_size("req")

    chosen = routes[0][:, :, None] == jnp.arange(experts_all, dtype=jnp.int32)
    expert_gates = jnp.sum(jnp.where(chosen, gate_weights[0][:, :, None], 0.0), axis=1)

    partial_out = attend(
        own_tokens,
        attn_gain,
        w_qkv,
        sink_logits.reshape(heads_dev, GROUP),
        w_out,
        kv_cache,
        page_table[0],
        cache_lengths,
    )
    return mixture(partial_out, own_tokens, moe_gain, expert_gates, w_gate_up, w_down)[None]


def solution(mesh):
    in_specs = (
        P("req", None, None),
        P(),
        P(None, "kv"),
        P("kv"),
        P("kv", None),
        P("req", None, "kv"),
        P("req", None),
        P("req"),
        P(),
        P("req", None, None),
        P("req", None, None),
        P("req", None, None, "kv"),
        P("req", "kv", None),
    )
    out_specs = P("req", "kv", None)
    return jax.shard_map(
        on_device, mesh=mesh, in_specs=in_specs, out_specs=out_specs, check_vma=False
    )
```

```python
import functools

import jax
import jax.numpy as jnp
import numpy as np
from jax import lax
from jax.experimental import pallas as pl
from jax.experimental.pallas import tpu as pltpu
from jax.sharding import PartitionSpec as P

HD = 64
GROUP = 8


THETA_BASE = 150000.0
EPSILON = 1e-05
ALPHA_GLU = 1.702


def rms_scale(row_data, gain_vector):
    row_data = row_data.astype(jnp.float32)
    mean_square = jnp.mean(row_data * row_data, axis=-1, keepdims=True)
    return row_data * lax.rsqrt(mean_square + EPSILON) * gain_vector


LANES = 2 * HD
PAGE_STEP = 8
FINITE = 1e37


def attend_kernel(
    pages_ref,
    length_ref,
    sink_ref,
    token_ref,
    gain_ref,
    frequency_ref,
    qkv_hbm,
    out_hbm,
    cache_hbm,
    partial_ref,
    natural_ref,
    qkv_ref,
    weight_ref,
    cache_ref,
    query_ref,
    total_ref,
    peak_ref,
    attended_ref,
    qkv_sem,
    weight_sem,
    cache_sem,
):
    heads, _, columns = query_ref.shape
    new_count = token_ref.shape[1]
    page_size = cache_hbm.shape[1]
    span = PAGE_STEP * page_size
    head_width = (GROUP + 2) * HD
    length = length_ref[0]
    chunks = (length + span - 1) // span
    whole_chunks = length // span

    def qkv_copy(head):
        part = slice(head * head_width, (head + 1) * head_width)
        return pltpu.make_async_copy(
            qkv_hbm.at[:, part], qkv_ref.at[:, part], qkv_sem.at[head]
        )

    weight_copy = pltpu.make_async_copy(out_hbm, weight_ref, weight_sem)
    for head in range(heads):
        qkv_copy(head).start()

    def fetch(chunk, _):
        for place in range(PAGE_STEP):
            at = chunk * PAGE_STEP + place
            pltpu.make_async_copy(
                cache_hbm.at[pages_ref[at]],
                cache_ref.at[pl.ds(pl.multiple_of(at * page_size, page_size), page_size)],
                cache_sem.at[chunk],
            ).start()
        return 0

    lax.fori_loop(0, chunks, fetch, 0)
    weight_copy.start()

    def key_side(block):
        lane = lax.broadcasted_iota(jnp.int32, block.shape, 1)
        return jnp.where(lane < HD, block, jnp.ones_like(block))

    def value_side(block):
        lane = lax.broadcasted_iota(jnp.int32, block.shape, 1)
        return jnp.where(lane < HD, jnp.ones_like(block), block)

    def weighted(block, weights):
        return lax.dot_general(
            block, weights, (((0,), (0,)), ((), ())), preferred_element_type=jnp.float32
        )

    tokens = token_ref[...].astype(jnp.float32).T
    natural_ref[...] = tokens.astype(jnp.bfloat16)
    normed = rms_scale(tokens, gain_ref[...][None]).astype(jnp.bfloat16)
    position = length + lax.broadcasted_iota(jnp.int32, (new_count, LANES), 0)
    angle = position.astype(jnp.float32) * frequency_ref[...]
    cosine = jnp.cos(angle)
    sine = jnp.sin(angle)
    lane = lax.broadcasted_iota(jnp.int32, (new_count, LANES), 1)
    sine = jnp.where(lane % HD < HD // 2, -sine, sine)

    def turned(block):
        swapped = jnp.where(
            lane % HD < HD // 2,
            pltpu.roll(block, LANES - HD // 2, 1),
            pltpu.roll(block, HD // 2, 1),
        )
        return block * cosine + swapped * sine

    key_at = lax.broadcasted_iota(jnp.int32, (new_count, columns), 0)
    query_at = lax.broadcasted_iota(jnp.int32, (new_count, columns), 1) % new_count
    causal = key_at <= query_at
    row = lax.broadcasted_iota(jnp.int32, (LANES, columns), 0)
    fresh_blocks = []
    for head in range(heads):
        qkv_copy(head).wait()
        projected = jnp.dot(
            normed,
            qkv_ref[:, head * head_width : (head + 1) * head_width],
            preferred_element_type=jnp.float32,
        )
        for pair in range(GROUP // 2):
            block = turned(projected[:, pair * LANES : (pair + 1) * LANES])
            block = (block * (HD**-0.5)).T.astype(jnp.bfloat16)
            for half in range(2):
                at = (2 * pair + half) * new_count
                query_ref[head, :HD, at : at + new_count] = block[half * HD : (half + 1) * HD]
        query_ref[head, HD:, :] = jnp.zeros((HD, columns), jnp.bfloat16)
        block = projected[:, GROUP * HD :]
        fresh_blocks.append(jnp.where(lane < HD, turned(block), block).astype(jnp.bfloat16))

    def begin(head):
        block = fresh_blocks[head]
        scores = jnp.dot(block, query_ref[head], preferred_element_type=jnp.float32)
        scores = jnp.where(causal, scores, -jnp.inf)
        sink = jnp.concatenate(
            [
                jnp.full((1, new_count), sink_ref[head * GROUP + place], jnp.float32)
                for place in range(GROUP)
            ],
            axis=1,
        )
        peak = jnp.maximum(sink, jnp.max(scores, axis=0, keepdims=True))
        weights = jnp.exp(scores - peak).astype(jnp.bfloat16)
        start = jnp.where(row < HD, jnp.exp(sink - peak), 0.0)
        total_ref[head] = start + weighted(value_side(block), weights)
        peak_ref[head : head + 1, :] = peak

    for head in range(heads):
        begin(head)
        peak = -peak_ref[head : head + 1, :]
        first = peak.astype(jnp.bfloat16).astype(jnp.float32)
        second = (peak - first).astype(jnp.bfloat16).astype(jnp.float32)
        third = peak - first - second
        tail_row = lax.broadcasted_iota(jnp.int32, (HD, columns), 0)
        shift = jnp.where(
            tail_row == 0,
            first,
            jnp.where(tail_row == 1, second, jnp.where(tail_row == 2, third, 0.0)),
        )
        query_ref[head, HD:, :] = shift.astype(jnp.bfloat16)

    def chunk_at(chunk):
        return pl.ds(pl.multiple_of(chunk * span, span), span)

    def absorb(chunk, masked):
        keys = cache_ref.at[chunk_at(chunk)]
        pltpu.make_async_copy(keys, keys, cache_sem.at[chunk]).wait()
        for head in range(heads):
            block = cache_ref[chunk_at(chunk), head * LANES : (head + 1) * LANES]
            scores = jnp.dot(
                key_side(block), query_ref[head], preferred_element_type=jnp.float32
            )
            weights = jnp.exp(scores)
            if masked:
                at = chunk * span + lax.broadcasted_iota(jnp.int32, scores.shape, 0)
                weights = jnp.where(at < length, weights, 0.0)
            total_ref[head] += weighted(value_side(block), weights.astype(jnp.bfloat16))

    def absorb_whole(chunk, _):
        absorb(chunk, False)
        return 0

    lax.fori_loop(0, whole_chunks, absorb_whole, 0)

    @pl.when(chunks > whole_chunks)
    def _():
        absorb(whole_chunks, True)

    largest = jnp.max(jnp.where(jnp.abs(total_ref[...]) < FINITE, 0.0, 1.0))

    @pl.when(largest > 0.5)
    def _():
        for head in range(heads):
            query_ref[head, HD:, :] = jnp.zeros((HD, columns), jnp.bfloat16)
        for head in range(heads):
            begin(head)

        def again(chunk, _):
            for head in range(heads):
                block = cache_ref[chunk_at(chunk), head * LANES : (head + 1) * LANES]
                scores = jnp.dot(block, query_ref[head], preferred_element_type=jnp.float32)
                at = chunk * span + lax.broadcasted_iota(jnp.int32, scores.shape, 0)
                scores = jnp.where(at < length, scores, -jnp.inf)
                old_peak = peak_ref[head : head + 1, :]
                peak = jnp.maximum(old_peak, jnp.max(scores, axis=0, keepdims=True))
                weights = jnp.exp(scores - peak).astype(jnp.bfloat16)
                total_ref[head] = total_ref[head] * jnp.exp(old_peak - peak) + weighted(
                    value_side(block), weights
                )
                peak_ref[head : head + 1, :] = peak
            return 0

        lax.fori_loop(0, chunks, again, 0)

    for head in range(heads):
        for pair in range(GROUP // 2):
            parts = []
            for half in range(2):
                at = (2 * pair + half) * new_count
                part = total_ref[head, :, at : at + new_count]
                parts.append(part[HD:] / part[0:1])
            block = jnp.concatenate(parts, axis=0).T.astype(jnp.bfloat16)
            at = head * GROUP * HD + pair * LANES
            attended_ref[:, at : at + LANES] = block
    weight_copy.wait()
    partial_ref[...] = lax.dot_general(
        attended_ref[...],
        weight_ref[...],
        (((1,), (1,)), ((), ())),
        preferred_element_type=jnp.float32,
    ).astype(jnp.bfloat16)


def attend(tokens, attn_gain, w_qkv, sink_logits, w_out, kv_cache, page_row, cached_length):
    new_count, width = tokens.shape
    heads = sink_logits.shape[0] // GROUP
    columns = GROUP * new_count
    pages, page_size, cache_width = kv_cache.shape
    frequency = THETA_BASE ** (-(np.arange(HD // 2) * 2.0 / HD))
    frequency = jnp.asarray(np.tile(frequency, 4)[None], jnp.float32)
    scalars = pl.BlockSpec(memory_space=pltpu.SMEM)
    dense = pl.BlockSpec(memory_space=pltpu.VMEM)
    apart = pl.BlockSpec(memory_space=pl.ANY)
    return pl.pallas_call(
        attend_kernel,
        in_specs=[scalars, scalars, scalars, dense, dense, dense, apart, apart, apart],
        out_specs=[dense, dense],
        out_shape=[jax.ShapeDtypeStruct((new_count, width), jnp.bfloat16)] * 2,
        scratch_shapes=[
            pltpu.VMEM(w_qkv.shape, jnp.bfloat16),
            pltpu.VMEM(w_out.shape[::-1], jnp.bfloat16),
            pltpu.VMEM((pages * page_size, cache_width), jnp.bfloat16),
            pltpu.VMEM((heads, LANES, columns), jnp.bfloat16),
            pltpu.VMEM((heads, LANES, columns), jnp.float32),
            pltpu.VMEM((heads, columns), jnp.float32),
            pltpu.VMEM((new_count, heads * GROUP * HD), jnp.bfloat16),
            pltpu.SemaphoreType.DMA((heads,)),
            pltpu.SemaphoreType.DMA,
            pltpu.SemaphoreType.DMA((pages // PAGE_STEP,)),
        ],
        compiler_params=pltpu.CompilerParams(vmem_limit_bytes=56 * 1024 * 1024),
        name="attend",
    )(
        page_row,
        cached_length,
        sink_logits,
        tokens.T,
        attn_gain,
        frequency,
        w_qkv,
        w_out.T,
        kv_cache,
    )


def moe_kernel(
    partial_ref,
    token_ref,
    gain_ref,
    route_ref,
    gate_ref,
    up_hbm,
    down_hbm,
    out_ref,
    up_ref,
    down_ref,
    gathered_ref,
    mixed_ref,
    mate_ref,
    plane_ref,
    column_ref,
    share_ref,
    pair_ref,
    cross_ref,
    total_ref,
    residual_ref,
    hidden_ref,
    tail_ref,
    up_sem,
    down_sem,
    share_sem,
    cross_sem,
    gather_sem,
    gather_mate_sem,
    other_sem,
    mate_sem,
    plane_sem,
    column_sem,
    sent_sem,
    *,
    grid_z,
    grid_y,
    grid_x,
):
    req, kv = lax.axis_index("req"), lax.axis_index("kv")
    kv_count = 2 * grid_x
    z, y = req // grid_y, req % grid_y
    x, core = kv // 2, kv % 2
    blocks, rows, width = mixed_ref.shape
    last_tile = width // 128 * 128
    experts = up_hbm.shape[0]
    plane_blocks = grid_y * kv_count
    xs, ys = range(1, grid_x), range(1, grid_y)

    def at_kv(other):
        return (req, other)

    mate = at_kv(2 * x + 1 - core)

    def x_peer(step):
        return at_kv(2 * ((x + step) % grid_x) + core)

    def y_peer(step):
        return (z * grid_y + (y + step) % grid_y, kv)

    def z_peer(step):
        return (((z + step) % grid_z) * grid_y + y, kv)

    def origin(plane):
        return (z + grid_z - plane) % grid_z

    def block_at(plane, y_step, x_step, parity):
        row = origin(plane) * grid_y + (y + grid_y + y_step) % grid_y
        return row * kv_count + 2 * ((x + grid_x + x_step) % grid_x) + parity

    def remote(source, target, sent, received, device):
        return pltpu.make_async_remote_copy(
            src_ref=source,
            dst_ref=target,
            send_sem=sent,
            recv_sem=received,
            device_id=device,
            device_id_type=pl.DeviceIdType.MESH,
        )

    def arrived(block, received):
        pltpu.make_async_copy(block, block, received).wait()

    up_copies = [
        pltpu.make_async_copy(up_hbm.at[e], up_ref.at[e], up_sem.at[e]) for e in range(experts)
    ]
    down_copies = [
        pltpu.make_async_copy(down_hbm.at[e], down_ref.at[e], down_sem.at[e])
        for e in range(experts)
    ]
    for expert in range(experts):
        up_copies[expert].start()
        down_copies[expert].start()

    tail_width = gathered_ref.shape[2] - last_tile
    lead = width - last_tile
    every_expert = experts * (blocks // kv_count)
    expert_at = lax.broadcasted_iota(jnp.int32, (tail_width, gate_ref.shape[1]), 0) - lead
    upper_side = expert_at < every_expert
    expert_at = jnp.where(upper_side, expert_at, expert_at - every_expert)
    tail = jnp.zeros(expert_at.shape, jnp.float32)
    for turn in range(gate_ref.shape[0]):
        named = expert_at == route_ref[turn : turn + 1, :]
        tail = jnp.where(named, gate_ref[turn : turn + 1, :], tail)
    upper = tail.astype(jnp.bfloat16).astype(jnp.float32)
    tail_ref[...] = jnp.where(upper_side, upper, tail - upper).T.astype(jnp.bfloat16)

    barrier = pltpu.get_barrier_semaphore()
    partners = [at_kv((kv + step) % kv_count) for step in range(1, kv_count)]
    partners += [y_peer(step) for step in ys] + [z_peer(step) for step in range(1, grid_z)]
    for device in partners:
        pl.semaphore_signal(
            barrier, inc=1, device_id=device, device_id_type=pl.DeviceIdType.MESH
        )
    pl.semaphore_wait(barrier, len(partners))

    def row_block(index):
        return pl.ds(pl.multiple_of(index * rows, rows), rows)

    for step in list(xs) + [0]:
        column = (x + step) % grid_x
        remote(
            partial_ref.at[row_block(2 * column + 1 - core)],
            share_ref.at[step],
            sent_sem.at[0],
            share_sem.at[step],
            mate,
        ).start()
    for step in xs:
        arrived(share_ref.at[step], share_sem.at[step])
        pair = partial_ref[row_block(2 * ((x + step) % grid_x) + core)].astype(jnp.float32)
        pair += share_ref[step].astype(jnp.float32)
        pair_ref[step - 1] = pair.astype(jnp.bfloat16)
        remote(
            pair_ref.at[step - 1],
            cross_ref.at[step - 1],
            sent_sem.at[3],
            cross_sem.at[step - 1],
            x_peer(step),
        ).start()
    arrived(share_ref.at[0], share_sem.at[0])
    summed = partial_ref[row_block(kv)].astype(jnp.float32) + share_ref[0].astype(jnp.float32)
    for step in xs:
        arrived(cross_ref.at[step - 1], cross_sem.at[step - 1])
        summed += cross_ref[step - 1].astype(jnp.float32)
    residual = token_ref[row_block(kv)].astype(jnp.float32) + summed
    residual_ref[...] = residual
    own = block_at(0, 0, 0, core)
    gathered_ref[own, :, last_tile:] = tail_ref[row_block(kv)]
    gathered_ref[own, :, :width] = rms_scale(residual, gain_ref[...][None]).astype(jnp.bfloat16)

    middle = width // 256 * 128
    halves = (slice(0, middle), slice(middle, gathered_ref.shape[2]))

    def pass_on(block, received, device, part=None):
        ref = gathered_ref.at[block]
        if part is not None:
            ref = gathered_ref.at[block, :, part]
        remote(ref, ref, sent_sem.at[1], received, device).start()

    def column_send(step):
        pass_on(own, gather_sem.at[step, 0, 0], z_peer(step))

    def gather_own(plane):
        block = block_at(plane, 0, 0, core)

        @pl.when(plane > 0)
        def _():
            arrived(gathered_ref.at[block], gather_sem.at[plane, 0, 0])

        for j in xs:
            pass_on(block, gather_sem.at[plane, 0, j], x_peer(j))
        for i in ys:
            pass_on(block, gather_sem.at[plane, i, 0], y_peer(i))
        pass_on(block, gather_mate_sem.at[plane, 0, 0], mate)

        @pl.when(plane + 1 < grid_z)
        def _():
            column_send(plane + 1)

    def gather_near(plane):
        def take(i, j):
            block = block_at(plane, -i, -j, core)
            arrived(gathered_ref.at[block], gather_sem.at[plane, i, j])
            return block

        near_y = [take(i, 0) for i in ys]
        for i, block in zip(ys, near_y):
            for j in xs:
                pass_on(block, gather_sem.at[plane, i, j], x_peer(j), halves[0])
        near_x = [take(0, j) for j in xs]
        for j, block in zip(xs, near_x):
            for i in ys:
                pass_on(block, other_sem.at[plane, i, j], y_peer(i), halves[1])
        for i, block in zip(ys, near_y):
            pass_on(block, gather_mate_sem.at[plane, i, 0], mate)
        for j, block in zip(xs, near_x):
            pass_on(block, gather_mate_sem.at[plane, 0, j], mate)

    def gather_far(plane):
        for i in ys:
            for j in xs:
                block = block_at(plane, -i, -j, core)
                arrived(gathered_ref.at[block, :, halves[0]], gather_sem.at[plane, i, j])
                arrived(gathered_ref.at[block, :, halves[1]], other_sem.at[plane, i, j])
                pass_on(block, gather_mate_sem.at[plane, i, j], mate)

    def gather_last(plane):
        for i in range(grid_y):
            for j in range(grid_x):
                block = block_at(plane, -i, -j, 1 - core)
                arrived(gathered_ref.at[block], gather_mate_sem.at[plane, i, j])

    def raise_up(plane, expert):
        start = pl.multiple_of(origin(plane) * plane_blocks, plane_blocks)
        part = gathered_ref[pl.ds(start, plane_blocks), :, :width]
        part = part.reshape(plane_blocks * rows, width)

        def projected(which):
            return lax.dot_general(
                part,
                up_ref[expert, which],
                (((1,), (1,)), ((), ())),
                preferred_element_type=jnp.float32,
            )

        gate, up = projected(0), projected(1)
        gates = gathered_ref[pl.ds(start, plane_blocks), :, last_tile:].reshape(-1, 128)
        place = width - last_tile + req * experts + expert
        lane = lax.broadcasted_iota(jnp.int32, gates.shape, 1)
        choice = (lane == place) | (lane == place + experts * (blocks // kv_count))
        weight = jnp.sum(
            jnp.where(choice, gates.astype(jnp.float32), 0.0), axis=1, keepdims=True
        )
        hidden = gate * jax.nn.sigmoid(ALPHA_GLU * gate) * (up + 1.0) * weight
        hidden_ref[...] = hidden.astype(jnp.bfloat16)

    def lower(plane, expert):
        start = pl.multiple_of(origin(plane) * plane_blocks, plane_blocks)
        mixed = jnp.dot(hidden_ref[...], down_ref[expert], preferred_element_type=jnp.float32)

        @pl.when(expert == 0)
        def _():
            total_ref[...] = mixed

        @pl.when(expert > 0)
        def _():
            total_ref[...] += mixed

        @pl.when(expert == experts - 1)
        def _():
            mixed_ref[pl.ds(start, plane_blocks)] = (
                total_ref[...].astype(jnp.bfloat16).reshape(plane_blocks, rows, width)
            )

    sum_halves = (slice(0, middle), slice(middle, width))

    def hand_over(source, target, received, device):
        remote(source, target, sent_sem.at[2], received, device).start()

    def add_to(block, part, terms):
        value = mixed_ref[block, :, part].astype(jnp.float32)
        for term in terms:
            value += term[...].astype(jnp.float32)
        mixed_ref[block, :, part] = value.astype(jnp.bfloat16)

    every = slice(0, width)
    far = [(i, j) for i in ys for j in xs]
    side_x = [(0, j) for j in xs]
    side_y = [(i, 0) for i in ys]

    def sum_mate_send(plane):
        for i, j in far + side_x + side_y + [(0, 0)]:
            hand_over(
                mixed_ref.at[block_at(plane, i, j, 1 - core)],
                mate_ref.at[plane, i, j],
                mate_sem.at[plane, i, j],
                mate,
            )

    def plane_send(plane, i, j, turn, device):
        part = sum_halves[turn]
        hand_over(
            mixed_ref.at[block_at(plane, i, j, core), :, part],
            plane_ref.at[plane, i, j, :, part],
            plane_sem.at[turn, plane, i, j],
            device,
        )

    def plane_take(plane, i, j, turn):
        part = sum_halves[turn]
        arrived(plane_ref.at[plane, i, j, :, part], plane_sem.at[turn, plane, i, j])
        return plane_ref.at[plane, i, j, :, part]

    def sum_mate(plane):
        for i, j in far + side_x + side_y + [(0, 0)]:
            arrived(mate_ref.at[plane, i, j], mate_sem.at[plane, i, j])
            add_to(block_at(plane, i, j, core), every, [mate_ref.at[plane, i, j]])
            if j:
                plane_send(plane, i, j, 0, x_peer(j))
            if i:
                plane_send(plane, i, j, 1, y_peer(i))

    def sum_near(plane):
        for i in ys:
            terms = [plane_take(plane, i, j, 0) for j in xs]
            add_to(block_at(plane, i, 0, core), sum_halves[0], terms)
            plane_send(plane, i, 0, 0, y_peer(i))
        for j in xs:
            terms = [plane_take(plane, i, j, 1) for i in ys]
            add_to(block_at(plane, 0, j, core), sum_halves[1], terms)
            plane_send(plane, 0, j, 1, x_peer(j))
        terms = [plane_take(plane, 0, j, 0) for j in xs]
        add_to(block_at(plane, 0, 0, core), sum_halves[0], terms)
        terms = [plane_take(plane, i, 0, 1) for i in ys]
        add_to(block_at(plane, 0, 0, core), sum_halves[1], terms)

    def sum_far(plane):
        block = block_at(plane, 0, 0, core)
        add_to(block, sum_halves[0], [plane_take(plane, i, 0, 0) for i in ys])
        add_to(block, sum_halves[1], [plane_take(plane, 0, j, 1) for j in xs])

        for step in range(1, grid_z):

            @pl.when(plane == step)
            def _():
                hand_over(
                    mixed_ref.at[block],
                    column_ref.at[step - 1],
                    column_sem.at[step - 1],
                    z_peer(grid_z - step),
                )

    turns = experts * grid_z

    def run_at(turn, first, task, start=0):
        shifted = turn - first

        @pl.when(
            (shifted >= experts * start) & (shifted < turns) & (shifted % experts == 0)
        )
        def _():
            task(shifted // experts)

    gather_own(0)
    gather_near(0)
    if grid_z > 1:
        gather_own(1)
    gather_far(0)

    def advance(turn, _):
        run_at(turn, experts, sum_mate_send)
        run_at(turn, 1 - 2 * experts, gather_own, 2)
        run_at(turn, 5, sum_far)
        run_at(turn, 4, sum_near)
        run_at(turn, 0, gather_last)
        for expert in range(experts):

            @pl.when(turn == expert)
            def _():
                up_copies[expert].wait()
                down_copies[expert].wait()

        @pl.when(turn < turns)
        def _():
            raise_up(turn // experts, turn % experts)

        run_at(turn, -experts, gather_near, 1)
        run_at(turn, 1 - experts, gather_far, 1)
        run_at(turn, 2, sum_mate)

        @pl.when(turn < turns)
        def _():
            lower(turn // experts, turn % experts)

        return 0

    lax.fori_loop(0, 4 + turns, advance, 0)

    result = residual_ref[...] + mixed_ref[own].astype(jnp.float32)
    for step in range(1, grid_z):
        arrived(column_ref.at[step - 1], column_sem.at[step - 1])
        result += column_ref[step - 1].astype(jnp.float32)
    out_ref[...] = result.astype(jnp.bfloat16)
    arrived(share_ref, sent_sem.at[0])
    arrived(pair_ref, sent_sem.at[3])
    arrived(gathered_ref.at[: blocks - 1], sent_sem.at[1])
    arrived(mixed_ref.at[: blocks - 1], sent_sem.at[2])


def mixture(partial_out, tokens, moe_gain, routes, gate_weights, w_gate_up, w_down):
    kv_count, req_count = lax.axis_size("kv"), lax.axis_size("req")
    new_count, width = tokens.shape
    rows = new_count // kv_count
    experts, hidden = w_down.shape[:2]
    blocks = kv_count * req_count
    grid_x = kv_count // 2
    grid_z = 4 if req_count % 4 == 0 else req_count
    grid_y = req_count // grid_z
    dense = pl.BlockSpec(memory_space=pltpu.VMEM)
    apart = pl.BlockSpec(memory_space=pl.ANY)
    half = jnp.bfloat16
    last_tile = width // 128 * 128
    tail_width = width - last_tile + 2 * experts * req_count
    full_width = last_tile + tail_width + -tail_width % 128
    return pl.pallas_call(
        functools.partial(moe_kernel, grid_z=grid_z, grid_y=grid_y, grid_x=grid_x),
        in_specs=[dense, dense, dense, dense, dense, apart, apart],
        out_specs=dense,
        out_shape=jax.ShapeDtypeStruct((rows, width), half),
        scratch_shapes=[
            pltpu.VMEM((experts, 2, hidden, width), half),
            pltpu.VMEM(w_down.shape, half),
            pltpu.VMEM((blocks, rows, full_width), half),
            pltpu.VMEM((blocks, rows, width), half),
            pltpu.VMEM((grid_z, grid_y, grid_x, rows, width), half),
            pltpu.VMEM((grid_z, grid_y, grid_x, rows, width), half),
            pltpu.VMEM((grid_z - 1, rows, width), half),
            pltpu.VMEM((grid_x, rows, width), half),
            pltpu.VMEM((grid_x - 1, rows, width), half),
            pltpu.VMEM((grid_x - 1, rows, width), half),
            pltpu.VMEM((blocks // grid_z * rows, width), jnp.float32),
            pltpu.VMEM((rows, width), jnp.float32),
            pltpu.VMEM((blocks // grid_z * rows, hidden), half),
            pltpu.VMEM((new_count, full_width - last_tile), half),
            pltpu.SemaphoreType.DMA((experts,)),
            pltpu.SemaphoreType.DMA((experts,)),
            pltpu.SemaphoreType.DMA((grid_x,)),
            pltpu.SemaphoreType.DMA((grid_x - 1,)),
            pltpu.SemaphoreType.DMA((grid_z, grid_y, grid_x)),
            pltpu.SemaphoreType.DMA((grid_z, grid_y, grid_x)),
            pltpu.SemaphoreType.DMA((grid_z, grid_y, grid_x)),
            pltpu.SemaphoreType.DMA((grid_z, grid_y, grid_x)),
            pltpu.SemaphoreType.DMA((2, grid_z, grid_y, grid_x)),
            pltpu.SemaphoreType.DMA((grid_z - 1,)),
            pltpu.SemaphoreType.DMA((4,)),
        ],
        compiler_params=pltpu.CompilerParams(
            vmem_limit_bytes=63 * 1024 * 1024, collective_id=0, has_side_effects=True
        ),
        name="mixture",
    )(
        partial_out,
        tokens,
        moe_gain,
        routes.T,
        gate_weights.T,
        jnp.swapaxes(w_gate_up, 2, 3),
        w_down,
    )


def on_device(
    tokens,
    attn_gain,
    w_qkv,
    sink_logits,
    w_out,
    kv_cache,
    page_table,
    cache_lengths,
    moe_gain,
    routes,
    gate_weights,
    w_gate_up,
    w_down,
):
    partial_out, own_tokens = attend(
        tokens[0],
        attn_gain,
        w_qkv,
        sink_logits,
        w_out,
        kv_cache,
        page_table[0],
        cache_lengths,
    )
    return mixture(
        partial_out, own_tokens, moe_gain, routes[0], gate_weights[0], w_gate_up, w_down
    )[None]


def solution(mesh):
    in_specs = (
        P("req", None, None),
        P(),
        P(None, "kv"),
        P("kv"),
        P("kv", None),
        P("req", None, "kv"),
        P("req", None),
        P("req"),
        P(),
        P("req", None, None),
        P("req", None, None),
        P("req", None, None, "kv"),
        P("req", "kv", None),
    )
    out_specs = P("req", "kv", None)
    return jax.shard_map(
        on_device, mesh=mesh, in_specs=in_specs, out_specs=out_specs, check_vma=False
    )
```

```python
import functools

import jax
import jax.numpy as jnp
import numpy as np
from jax import lax
from jax.experimental import pallas as pl
from jax.experimental.pallas import tpu as pltpu
from jax.sharding import PartitionSpec as P

HD = 64
GROUP = 8


THETA_BASE = 150000.0
EPSILON = 1e-05
ALPHA_GLU = 1.702


def rms_scale(row_data, gain_vector):
    row_data = row_data.astype(jnp.float32)
    mean_square = jnp.mean(row_data * row_data, axis=-1, keepdims=True)
    return row_data * lax.rsqrt(mean_square + EPSILON) * gain_vector


LANES = 2 * HD
PAGE_STEP = 8
FINITE = 1e37


def attend_kernel(
    pages_ref,
    length_ref,
    sink_ref,
    token_ref,
    gain_ref,
    frequency_ref,
    qkv_hbm,
    out_hbm,
    cache_hbm,
    partial_ref,
    own_ref,
    natural_ref,
    qkv_ref,
    weight_ref,
    cache_ref,
    query_ref,
    total_ref,
    peak_ref,
    attended_ref,
    qkv_sem,
    weight_sem,
    cache_sem,
):
    heads, _, columns = query_ref.shape
    new_count = token_ref.shape[1]
    page_size = cache_hbm.shape[1]
    span = PAGE_STEP * page_size
    head_width = (GROUP + 2) * HD
    length = length_ref[0]
    chunks = (length + span - 1) // span
    whole_chunks = length // span

    def qkv_copy(head):
        part = slice(head * head_width, (head + 1) * head_width)
        return pltpu.make_async_copy(
            qkv_hbm.at[:, part], qkv_ref.at[:, part], qkv_sem.at[head]
        )

    weight_copy = pltpu.make_async_copy(out_hbm, weight_ref, weight_sem)
    for head in range(heads):
        qkv_copy(head).start()

    def fetch(chunk, _):
        for place in range(PAGE_STEP):
            at = chunk * PAGE_STEP + place
            pltpu.make_async_copy(
                cache_hbm.at[pages_ref[at]],
                cache_ref.at[pl.ds(pl.multiple_of(at * page_size, page_size), page_size)],
                cache_sem.at[chunk],
            ).start()
        return 0

    lax.fori_loop(0, chunks, fetch, 0)
    weight_copy.start()

    def key_side(block):
        lane = lax.broadcasted_iota(jnp.int32, block.shape, 1)
        return jnp.where(lane < HD, block, jnp.ones_like(block))

    def value_side(block):
        lane = lax.broadcasted_iota(jnp.int32, block.shape, 1)
        return jnp.where(lane < HD, jnp.ones_like(block), block)

    def weighted(block, weights):
        return lax.dot_general(
            block, weights, (((0,), (0,)), ((), ())), preferred_element_type=jnp.float32
        )

    tokens = token_ref[...].astype(jnp.float32).T
    natural_ref[...] = tokens.astype(jnp.bfloat16)
    rows = own_ref.shape[0]
    own_at = pl.multiple_of(lax.axis_index("kv") * rows, rows)
    own_ref[...] = natural_ref[pl.ds(own_at, rows)]
    normed = rms_scale(tokens, gain_ref[...][None]).astype(jnp.bfloat16)
    position = length + lax.broadcasted_iota(jnp.int32, (new_count, LANES), 0)
    angle = position.astype(jnp.float32) * frequency_ref[...]
    cosine = jnp.cos(angle)
    sine = jnp.sin(angle)
    lane = lax.broadcasted_iota(jnp.int32, (new_count, LANES), 1)
    sine = jnp.where(lane % HD < HD // 2, -sine, sine)

    def turned(block):
        swapped = jnp.where(
            lane % HD < HD // 2,
            pltpu.roll(block, LANES - HD // 2, 1),
            pltpu.roll(block, HD // 2, 1),
        )
        return block * cosine + swapped * sine

    key_at = lax.broadcasted_iota(jnp.int32, (new_count, columns), 0)
    query_at = lax.broadcasted_iota(jnp.int32, (new_count, columns), 1) % new_count
    causal = key_at <= query_at
    row = lax.broadcasted_iota(jnp.int32, (LANES, columns), 0)
    fresh_blocks = []
    for head in range(heads):
        qkv_copy(head).wait()
        projected = jnp.dot(
            normed,
            qkv_ref[:, head * head_width : (head + 1) * head_width],
            preferred_element_type=jnp.float32,
        )
        for pair in range(GROUP // 2):
            block = turned(projected[:, pair * LANES : (pair + 1) * LANES])
            block = (block * (HD**-0.5)).T.astype(jnp.bfloat16)
            for half in range(2):
                at = (2 * pair + half) * new_count
                query_ref[head, :HD, at : at + new_count] = block[half * HD : (half + 1) * HD]
        query_ref[head, HD:, :] = jnp.zeros((HD, columns), jnp.bfloat16)
        block = projected[:, GROUP * HD :]
        fresh_blocks.append(jnp.where(lane < HD, turned(block), block).astype(jnp.bfloat16))

    def begin(head):
        block = fresh_blocks[head]
        scores = jnp.dot(block, query_ref[head], preferred_element_type=jnp.float32)
        scores = jnp.where(causal, scores, -jnp.inf)
        sink = jnp.concatenate(
            [
                jnp.full((1, new_count), sink_ref[head * GROUP + place], jnp.float32)
                for place in range(GROUP)
            ],
            axis=1,
        )
        peak = jnp.maximum(sink, jnp.max(scores, axis=0, keepdims=True))
        weights = jnp.exp(scores - peak).astype(jnp.bfloat16)
        start = jnp.where(row < HD, jnp.exp(sink - peak), 0.0)
        total_ref[head] = start + weighted(value_side(block), weights)
        peak_ref[head : head + 1, :] = peak

    for head in range(heads):
        begin(head)
        peak = -peak_ref[head : head + 1, :]
        first = peak.astype(jnp.bfloat16).astype(jnp.float32)
        second = (peak - first).astype(jnp.bfloat16).astype(jnp.float32)
        third = peak - first - second
        tail_row = lax.broadcasted_iota(jnp.int32, (HD, columns), 0)
        shift = jnp.where(
            tail_row == 0,
            first,
            jnp.where(tail_row == 1, second, jnp.where(tail_row == 2, third, 0.0)),
        )
        query_ref[head, HD:, :] = shift.astype(jnp.bfloat16)

    def chunk_at(chunk):
        return pl.ds(pl.multiple_of(chunk * span, span), span)

    def absorb(chunk, masked):
        keys = cache_ref.at[chunk_at(chunk)]
        pltpu.make_async_copy(keys, keys, cache_sem.at[chunk]).wait()
        for head in range(heads):
            block = cache_ref[chunk_at(chunk), head * LANES : (head + 1) * LANES]
            scores = jnp.dot(
                key_side(block), query_ref[head], preferred_element_type=jnp.float32
            )
            weights = jnp.exp(scores)
            if masked:
                at = chunk * span + lax.broadcasted_iota(jnp.int32, scores.shape, 0)
                weights = jnp.where(at < length, weights, 0.0)
            total_ref[head] += weighted(value_side(block), weights.astype(jnp.bfloat16))

    def absorb_whole(chunk, _):
        absorb(chunk, False)
        return 0

    lax.fori_loop(0, whole_chunks, absorb_whole, 0)

    @pl.when(chunks > whole_chunks)
    def _():
        absorb(whole_chunks, True)

    largest = jnp.max(jnp.where(jnp.abs(total_ref[...]) < FINITE, 0.0, 1.0))

    @pl.when(largest > 0.5)
    def _():
        for head in range(heads):
            query_ref[head, HD:, :] = jnp.zeros((HD, columns), jnp.bfloat16)
        for head in range(heads):
            begin(head)

        def again(chunk, _):
            for head in range(heads):
                block = cache_ref[chunk_at(chunk), head * LANES : (head + 1) * LANES]
                scores = jnp.dot(block, query_ref[head], preferred_element_type=jnp.float32)
                at = chunk * span + lax.broadcasted_iota(jnp.int32, scores.shape, 0)
                scores = jnp.where(at < length, scores, -jnp.inf)
                old_peak = peak_ref[head : head + 1, :]
                peak = jnp.maximum(old_peak, jnp.max(scores, axis=0, keepdims=True))
                weights = jnp.exp(scores - peak).astype(jnp.bfloat16)
                total_ref[head] = total_ref[head] * jnp.exp(old_peak - peak) + weighted(
                    value_side(block), weights
                )
                peak_ref[head : head + 1, :] = peak
            return 0

        lax.fori_loop(0, chunks, again, 0)

    for head in range(heads):
        for pair in range(GROUP // 2):
            parts = []
            for half in range(2):
                at = (2 * pair + half) * new_count
                part = total_ref[head, :, at : at + new_count]
                parts.append(part[HD:] / part[0:1])
            block = jnp.concatenate(parts, axis=0).T.astype(jnp.bfloat16)
            at = head * GROUP * HD + pair * LANES
            attended_ref[:, at : at + LANES] = block
    weight_copy.wait()
    partial_ref[...] = lax.dot_general(
        attended_ref[...],
        weight_ref[...],
        (((1,), (1,)), ((), ())),
        preferred_element_type=jnp.float32,
    ).astype(jnp.bfloat16)


def attend(tokens, attn_gain, w_qkv, sink_logits, w_out, kv_cache, page_row, cached_length):
    new_count, width = tokens.shape
    heads = sink_logits.shape[0] // GROUP
    columns = GROUP * new_count
    pages, page_size, cache_width = kv_cache.shape
    frequency = THETA_BASE ** (-(np.arange(HD // 2) * 2.0 / HD))
    frequency = jnp.asarray(np.tile(frequency, 4)[None], jnp.float32)
    scalars = pl.BlockSpec(memory_space=pltpu.SMEM)
    dense = pl.BlockSpec(memory_space=pltpu.VMEM)
    apart = pl.BlockSpec(memory_space=pl.ANY)
    return pl.pallas_call(
        attend_kernel,
        in_specs=[scalars, scalars, scalars, dense, dense, dense, apart, apart, apart],
        out_specs=[dense, dense],
        out_shape=[
            jax.ShapeDtypeStruct((new_count, width), jnp.bfloat16),
            jax.ShapeDtypeStruct((new_count // lax.axis_size("kv"), width), jnp.bfloat16),
        ],
        scratch_shapes=[
            pltpu.VMEM((new_count, width), jnp.bfloat16),
            pltpu.VMEM(w_qkv.shape, jnp.bfloat16),
            pltpu.VMEM(w_out.shape[::-1], jnp.bfloat16),
            pltpu.VMEM((pages * page_size, cache_width), jnp.bfloat16),
            pltpu.VMEM((heads, LANES, columns), jnp.bfloat16),
            pltpu.VMEM((heads, LANES, columns), jnp.float32),
            pltpu.VMEM((heads, columns), jnp.float32),
            pltpu.VMEM((new_count, heads * GROUP * HD), jnp.bfloat16),
            pltpu.SemaphoreType.DMA((heads,)),
            pltpu.SemaphoreType.DMA,
            pltpu.SemaphoreType.DMA((pages // PAGE_STEP,)),
        ],
        compiler_params=pltpu.CompilerParams(vmem_limit_bytes=56 * 1024 * 1024),
        name="attend",
    )(
        page_row,
        cached_length,
        sink_logits,
        tokens.T,
        attn_gain,
        frequency,
        w_qkv,
        w_out.T,
        kv_cache,
    )


def moe_kernel(
    partial_ref,
    token_ref,
    gain_ref,
    route_ref,
    gate_ref,
    up_hbm,
    down_hbm,
    out_ref,
    up_ref,
    down_ref,
    gathered_ref,
    mixed_ref,
    mate_ref,
    plane_ref,
    column_ref,
    share_ref,
    pair_ref,
    cross_ref,
    residual_ref,
    hidden_ref,
    tail_ref,
    up_sem,
    down_sem,
    share_sem,
    cross_sem,
    gather_sem,
    gather_mate_sem,
    other_sem,
    mate_sem,
    plane_sem,
    column_sem,
    sent_sem,
    *,
    grid_z,
    grid_y,
    grid_x,
):
    req, kv = lax.axis_index("req"), lax.axis_index("kv")
    kv_count = 2 * grid_x
    z, y = req // grid_y, req % grid_y
    x, core = kv // 2, kv % 2
    blocks, rows, width = mixed_ref.shape
    last_tile = width // 128 * 128
    experts = up_hbm.shape[0]
    plane_blocks = grid_y * kv_count
    xs, ys = range(1, grid_x), range(1, grid_y)

    def at_kv(other):
        return (req, other)

    mate = at_kv(2 * x + 1 - core)

    def x_peer(step):
        return at_kv(2 * ((x + step) % grid_x) + core)

    def y_peer(step):
        return (z * grid_y + (y + step) % grid_y, kv)

    def z_peer(step):
        return (((z + step) % grid_z) * grid_y + y, kv)

    def origin(plane):
        return (z + grid_z - plane) % grid_z

    def block_at(plane, y_step, x_step, parity):
        row = origin(plane) * grid_y + (y + grid_y + y_step) % grid_y
        return row * kv_count + 2 * ((x + grid_x + x_step) % grid_x) + parity

    def remote(source, target, sent, received, device):
        return pltpu.make_async_remote_copy(
            src_ref=source,
            dst_ref=target,
            send_sem=sent,
            recv_sem=received,
            device_id=device,
            device_id_type=pl.DeviceIdType.MESH,
        )

    def arrived(block, received):
        pltpu.make_async_copy(block, block, received).wait()

    up_copies = [
        pltpu.make_async_copy(up_hbm.at[e], up_ref.at[e], up_sem.at[e]) for e in range(experts)
    ]
    down_copies = [
        pltpu.make_async_copy(down_hbm.at[e], down_ref.at[e], down_sem.at[e])
        for e in range(experts)
    ]
    for expert in range(experts):
        up_copies[expert].start()
        down_copies[expert].start()

    tail_width = gathered_ref.shape[2] - last_tile
    lead = width - last_tile
    every_expert = experts * (blocks // kv_count)
    expert_at = lax.broadcasted_iota(jnp.int32, (tail_width, gate_ref.shape[1]), 0) - lead
    upper_side = expert_at < every_expert
    expert_at = jnp.where(upper_side, expert_at, expert_at - every_expert)
    tail = jnp.zeros(expert_at.shape, jnp.float32)
    for turn in range(gate_ref.shape[0]):
        named = expert_at == route_ref[turn : turn + 1, :]
        tail = jnp.where(named, gate_ref[turn : turn + 1, :], tail)
    upper = tail.astype(jnp.bfloat16).astype(jnp.float32)
    tail_ref[...] = jnp.where(upper_side, upper, tail - upper).T.astype(jnp.bfloat16)

    barrier = pltpu.get_barrier_semaphore()
    partners = [at_kv((kv + step) % kv_count) for step in range(1, kv_count)]
    partners += [y_peer(step) for step in ys] + [z_peer(step) for step in range(1, grid_z)]
    for device in partners:
        pl.semaphore_signal(
            barrier, inc=1, device_id=device, device_id_type=pl.DeviceIdType.MESH
        )
    pl.semaphore_wait(barrier, len(partners))

    def row_block(index):
        return pl.ds(pl.multiple_of(index * rows, rows), rows)

    for step in list(xs) + [0]:
        column = (x + step) % grid_x
        remote(
            partial_ref.at[row_block(2 * column + 1 - core)],
            share_ref.at[step],
            sent_sem.at[0],
            share_sem.at[step],
            mate,
        ).start()
    for step in xs:
        arrived(share_ref.at[step], share_sem.at[step])
        pair = partial_ref[row_block(2 * ((x + step) % grid_x) + core)].astype(jnp.float32)
        pair += share_ref[step].astype(jnp.float32)
        pair_ref[step - 1] = pair.astype(jnp.bfloat16)
        remote(
            pair_ref.at[step - 1],
            cross_ref.at[step - 1],
            sent_sem.at[3],
            cross_sem.at[step - 1],
            x_peer(step),
        ).start()
    arrived(share_ref.at[0], share_sem.at[0])
    summed = partial_ref[row_block(kv)].astype(jnp.float32) + share_ref[0].astype(jnp.float32)
    for step in xs:
        arrived(cross_ref.at[step - 1], cross_sem.at[step - 1])
        summed += cross_ref[step - 1].astype(jnp.float32)
    residual = token_ref[...].astype(jnp.float32) + summed
    residual_ref[...] = residual
    own = block_at(0, 0, 0, core)
    gathered_ref[own, :, last_tile:] = tail_ref[row_block(kv)]
    gathered_ref[own, :, :width] = rms_scale(residual, gain_ref[...][None]).astype(jnp.bfloat16)

    middle = width // 256 * 128
    halves = (slice(0, middle), slice(middle, gathered_ref.shape[2]))

    def pass_on(block, received, device, part=None):
        ref = gathered_ref.at[block]
        if part is not None:
            ref = gathered_ref.at[block, :, part]
        remote(ref, ref, sent_sem.at[1], received, device).start()

    def gather_own(plane):
        block = block_at(plane, 0, 0, core)

        @pl.when(plane > 0)
        def _():
            arrived(gathered_ref.at[block], gather_sem.at[plane, 0, 0])

        for j in xs:
            pass_on(block, gather_sem.at[plane, 0, j], x_peer(j))
        for i in ys:
            pass_on(block, gather_sem.at[plane, i, 0], y_peer(i))
        pass_on(block, gather_mate_sem.at[plane, 0, 0], mate)

        @pl.when(plane + 1 < grid_z)
        def _():
            pass_on(block, gather_sem.at[plane + 1, 0, 0], z_peer(1))

    def gather_near(plane):
        def take(i, j):
            block = block_at(plane, -i, -j, core)
            arrived(gathered_ref.at[block], gather_sem.at[plane, i, j])
            return block

        near_y = [take(i, 0) for i in ys]
        for i, block in zip(ys, near_y):
            for j in xs:
                pass_on(block, gather_sem.at[plane, i, j], x_peer(j), halves[0])
        near_x = [take(0, j) for j in xs]
        for j, block in zip(xs, near_x):
            for i in ys:
                pass_on(block, other_sem.at[plane, i, j], y_peer(i), halves[1])
        for i, block in zip(ys, near_y):
            pass_on(block, gather_mate_sem.at[plane, i, 0], mate)
        for j, block in zip(xs, near_x):
            pass_on(block, gather_mate_sem.at[plane, 0, j], mate)

    def gather_far(plane):
        for i in ys:
            for j in xs:
                block = block_at(plane, -i, -j, core)
                arrived(gathered_ref.at[block, :, halves[0]], gather_sem.at[plane, i, j])
                arrived(gathered_ref.at[block, :, halves[1]], other_sem.at[plane, i, j])
                pass_on(block, gather_mate_sem.at[plane, i, j], mate)

    def gather_last(plane):
        for i in range(grid_y):
            for j in range(grid_x):
                block = block_at(plane, -i, -j, 1 - core)
                arrived(gathered_ref.at[block], gather_mate_sem.at[plane, i, j])

    def raise_up(plane, expert):
        start = pl.multiple_of(origin(plane) * plane_blocks, plane_blocks)
        part = gathered_ref[pl.ds(start, plane_blocks), :, :width]
        part = part.reshape(plane_blocks * rows, width)

        def projected(which):
            return lax.dot_general(
                part,
                up_ref[expert, which],
                (((1,), (1,)), ((), ())),
                preferred_element_type=jnp.float32,
            )

        gate, up = projected(0), projected(1)
        gates = gathered_ref[pl.ds(start, plane_blocks), :, last_tile:].reshape(-1, 128)
        place = width - last_tile + req * experts + expert
        lane = lax.broadcasted_iota(jnp.int32, gates.shape, 1)
        choice = (lane == place) | (lane == place + experts * (blocks // kv_count))
        weight = jnp.sum(
            jnp.where(choice, gates.astype(jnp.float32), 0.0), axis=1, keepdims=True
        )
        hidden = gate * jax.nn.sigmoid(ALPHA_GLU * gate) * (up + 1.0) * weight
        hidden_ref[expert] = hidden.astype(jnp.bfloat16)

    sum_halves = (slice(0, middle), slice(middle, width))

    def hand_over(source, target, received, device):
        remote(source, target, sent_sem.at[2], received, device).start()

    def add_to(block, part, terms):
        value = mixed_ref[block, :, part].astype(jnp.float32)
        for term in terms:
            value += term[...].astype(jnp.float32)
        mixed_ref[block, :, part] = value.astype(jnp.bfloat16)

    far = [(i, j) for i in ys for j in xs]
    side_x = [(0, j) for j in xs]
    side_y = [(i, 0) for i in ys]

    def lower(plane):
        start = pl.multiple_of(origin(plane) * plane_blocks, plane_blocks)
        for turn, part in enumerate(sum_halves):
            mixed = jnp.dot(
                hidden_ref[0], down_ref[0, :, part], preferred_element_type=jnp.float32
            )
            for expert in range(1, experts):
                mixed += jnp.dot(
                    hidden_ref[expert],
                    down_ref[expert, :, part],
                    preferred_element_type=jnp.float32,
                )
            mixed_ref[pl.ds(start, plane_blocks), :, part] = mixed.astype(jnp.bfloat16).reshape(
                plane_blocks, rows, part.stop - part.start
            )
            for i, j in far + side_x + side_y + [(0, 0)]:
                hand_over(
                    mixed_ref.at[block_at(plane, i, j, 1 - core), :, part],
                    mate_ref.at[plane, i, j, :, part],
                    mate_sem.at[turn, plane, i, j],
                    mate,
                )

    def plane_send(plane, i, j, turn, device):
        part = sum_halves[turn]
        hand_over(
            mixed_ref.at[block_at(plane, i, j, core), :, part],
            plane_ref.at[plane, i, j, :, part],
            plane_sem.at[turn, plane, i, j],
            device,
        )

    def plane_take(plane, i, j, turn):
        part = sum_halves[turn]
        arrived(plane_ref.at[plane, i, j, :, part], plane_sem.at[turn, plane, i, j])
        return plane_ref.at[plane, i, j, :, part]

    def sum_mate(plane):
        for turn, part in enumerate(sum_halves):
            for i, j in far + (side_y + side_x if turn else side_x + side_y) + [(0, 0)]:
                term = mate_ref.at[plane, i, j, :, part]
                arrived(term, mate_sem.at[turn, plane, i, j])
                add_to(block_at(plane, i, j, core), part, [term])
                if j and turn == 0:
                    plane_send(plane, i, j, 0, x_peer(j))
                if i and turn == 1:
                    plane_send(plane, i, j, 1, y_peer(i))

    def sum_near(plane):
        for i in ys:
            terms = [plane_take(plane, i, j, 0) for j in xs]
            add_to(block_at(plane, i, 0, core), sum_halves[0], terms)
            plane_send(plane, i, 0, 0, y_peer(i))
        for j in xs:
            terms = [plane_take(plane, i, j, 1) for i in ys]
            add_to(block_at(plane, 0, j, core), sum_halves[1], terms)
            plane_send(plane, 0, j, 1, x_peer(j))
        terms = [plane_take(plane, 0, j, 0) for j in xs]
        add_to(block_at(plane, 0, 0, core), sum_halves[0], terms)
        terms = [plane_take(plane, i, 0, 1) for i in ys]
        add_to(block_at(plane, 0, 0, core), sum_halves[1], terms)

    def sum_far(plane):
        block = block_at(plane, 0, 0, core)
        add_to(block, sum_halves[0], [plane_take(plane, i, 0, 0) for i in ys])
        add_to(block, sum_halves[1], [plane_take(plane, 0, j, 1) for j in xs])

        for step in range(1, grid_z):

            @pl.when(plane == step)
            def _():
                hand_over(
                    mixed_ref.at[block],
                    column_ref.at[step - 1],
                    column_sem.at[step - 1],
                    z_peer(grid_z - step),
                )

    turns = experts * grid_z

    def run_at(turn, first, task, start=0):
        shifted = turn - first

        @pl.when(
            (shifted >= experts * start) & (shifted < turns) & (shifted % experts == 0)
        )
        def _():
            task(shifted // experts)

    gather_own(0)
    gather_near(0)
    if grid_z > 1:
        gather_own(1)
    gather_far(0)

    def advance(turn, _):
        run_at(turn, 6, sum_far)
        run_at(turn, 5, sum_near)
        run_at(turn, -2, gather_near, 2)
        run_at(turn, 0, gather_last)
        run_at(turn, -4, gather_own, 2)

        @pl.when(turn == 1)
        def _():
            gather_near(1)

        run_at(turn, 3, sum_mate)
        for expert in range(experts):

            @pl.when(turn == expert)
            def _():
                up_copies[expert].wait()
                down_copies[expert].wait()

        @pl.when(turn < turns)
        def _():
            raise_up(turn // experts, turn % experts)

        run_at(turn, -1, gather_far, 1)

        @pl.when((turn < turns) & (turn % experts == experts - 1))
        def _():
            lower(turn // experts)

        return 0

    lax.fori_loop(0, 5 + turns, advance, 0)

    result = residual_ref[...] + mixed_ref[own].astype(jnp.float32)
    for step in range(1, grid_z):
        arrived(column_ref.at[step - 1], column_sem.at[step - 1])
        result += column_ref[step - 1].astype(jnp.float32)
    out_ref[...] = result.astype(jnp.bfloat16)
    arrived(share_ref, sent_sem.at[0])
    arrived(pair_ref, sent_sem.at[3])
    arrived(gathered_ref.at[: blocks - 1], sent_sem.at[1])
    arrived(mixed_ref.at[: blocks - 1], sent_sem.at[2])


def mixture(partial_out, tokens, moe_gain, routes, gate_weights, w_gate_up, w_down):
    kv_count, req_count = lax.axis_size("kv"), lax.axis_size("req")
    new_count, width = partial_out.shape
    rows = new_count // kv_count
    experts, hidden = w_down.shape[:2]
    blocks = kv_count * req_count
    grid_x = kv_count // 2
    grid_z = 4 if req_count % 4 == 0 else req_count
    grid_y = req_count // grid_z
    dense = pl.BlockSpec(memory_space=pltpu.VMEM)
    apart = pl.BlockSpec(memory_space=pl.ANY)
    half = jnp.bfloat16
    last_tile = width // 128 * 128
    tail_width = width - last_tile + 2 * experts * req_count
    full_width = last_tile + tail_width + -tail_width % 128
    return pl.pallas_call(
        functools.partial(moe_kernel, grid_z=grid_z, grid_y=grid_y, grid_x=grid_x),
        in_specs=[dense, dense, dense, dense, dense, apart, apart],
        out_specs=dense,
        out_shape=jax.ShapeDtypeStruct((rows, width), half),
        scratch_shapes=[
            pltpu.VMEM((experts, 2, hidden, width), half),
            pltpu.VMEM(w_down.shape, half),
            pltpu.VMEM((blocks, rows, full_width), half),
            pltpu.VMEM((blocks, rows, width), half),
            pltpu.VMEM((grid_z, grid_y, grid_x, rows, width), half),
            pltpu.VMEM((grid_z, grid_y, grid_x, rows, width), half),
            pltpu.VMEM((grid_z - 1, rows, width), half),
            pltpu.VMEM((grid_x, rows, width), half),
            pltpu.VMEM((grid_x - 1, rows, width), half),
            pltpu.VMEM((grid_x - 1, rows, width), half),
            pltpu.VMEM((rows, width), jnp.float32),
            pltpu.VMEM((experts, blocks // grid_z * rows, hidden), half),
            pltpu.VMEM((new_count, full_width - last_tile), half),
            pltpu.SemaphoreType.DMA((experts,)),
            pltpu.SemaphoreType.DMA((experts,)),
            pltpu.SemaphoreType.DMA((grid_x,)),
            pltpu.SemaphoreType.DMA((grid_x - 1,)),
            pltpu.SemaphoreType.DMA((grid_z, grid_y, grid_x)),
            pltpu.SemaphoreType.DMA((grid_z, grid_y, grid_x)),
            pltpu.SemaphoreType.DMA((grid_z, grid_y, grid_x)),
            pltpu.SemaphoreType.DMA((2, grid_z, grid_y, grid_x)),
            pltpu.SemaphoreType.DMA((2, grid_z, grid_y, grid_x)),
            pltpu.SemaphoreType.DMA((grid_z - 1,)),
            pltpu.SemaphoreType.DMA((4,)),
        ],
        compiler_params=pltpu.CompilerParams(
            vmem_limit_bytes=63 * 1024 * 1024, collective_id=0, has_side_effects=True
        ),
        name="mixture",
    )(
        partial_out,
        tokens,
        moe_gain,
        routes.T,
        gate_weights.T,
        jnp.swapaxes(w_gate_up, 2, 3),
        w_down,
    )


def on_device(
    tokens,
    attn_gain,
    w_qkv,
    sink_logits,
    w_out,
    kv_cache,
    page_table,
    cache_lengths,
    moe_gain,
    routes,
    gate_weights,
    w_gate_up,
    w_down,
):
    partial_out, own_tokens = attend(
        tokens[0],
        attn_gain,
        w_qkv,
        sink_logits,
        w_out,
        kv_cache,
        page_table[0],
        cache_lengths,
    )
    return mixture(
        partial_out, own_tokens, moe_gain, routes[0], gate_weights[0], w_gate_up, w_down
    )[None]


def solution(mesh):
    in_specs = (
        P("req", None, None),
        P(),
        P(None, "kv"),
        P("kv"),
        P("kv", None),
        P("req", None, "kv"),
        P("req", None),
        P("req"),
        P(),
        P("req", None, None),
        P("req", None, None),
        P("req", None, None, "kv"),
        P("req", "kv", None),
    )
    out_specs = P("req", "kv", None)
    return jax.shard_map(
        on_device, mesh=mesh, in_specs=in_specs, out_specs=out_specs, check_vma=False
    )
```

```python
import functools

import jax
import jax.numpy as jnp
import numpy as np
from jax import lax
from jax.experimental import pallas as pl
from jax.experimental.pallas import tpu as pltpu
from jax.sharding import PartitionSpec as P

HD = 64
GROUP = 8


THETA_BASE = 150000.0
EPSILON = 1e-05
ALPHA_GLU = 1.702


def rms_scale(row_data, gain_vector):
    row_data = row_data.astype(jnp.float32)
    mean_square = jnp.mean(row_data * row_data, axis=-1, keepdims=True)
    return row_data * lax.rsqrt(mean_square + EPSILON) * gain_vector


LANES = 2 * HD
PAGE_STEP = 8
FINITE = 1e37


def attend_kernel(
    pages_ref,
    length_ref,
    sink_ref,
    token_ref,
    gain_ref,
    frequency_ref,
    qkv_hbm,
    out_hbm,
    cache_hbm,
    partial_ref,
    own_ref,
    natural_ref,
    qkv_ref,
    weight_ref,
    cache_ref,
    query_ref,
    total_ref,
    peak_ref,
    attended_ref,
    qkv_sem,
    weight_sem,
    cache_sem,
):
    heads, _, columns = query_ref.shape
    new_count = token_ref.shape[1]
    page_size = cache_hbm.shape[1]
    span = PAGE_STEP * page_size
    head_width = (GROUP + 2) * HD
    length = length_ref[0]
    chunks = (length + span - 1) // span
    whole_chunks = length // span

    def qkv_copy(head):
        part = slice(head * head_width, (head + 1) * head_width)
        return pltpu.make_async_copy(
            qkv_hbm.at[:, part], qkv_ref.at[:, part], qkv_sem.at[head]
        )

    weight_copy = pltpu.make_async_copy(out_hbm, weight_ref, weight_sem)
    for head in range(heads):
        qkv_copy(head).start()

    def fetch(chunk, _):
        for place in range(PAGE_STEP):
            at = chunk * PAGE_STEP + place
            pltpu.make_async_copy(
                cache_hbm.at[pages_ref[at]],
                cache_ref.at[pl.ds(pl.multiple_of(at * page_size, page_size), page_size)],
                cache_sem.at[chunk],
            ).start()
        return 0

    lax.fori_loop(0, chunks, fetch, 0)
    weight_copy.start()

    def key_side(block):
        lane = lax.broadcasted_iota(jnp.int32, block.shape, 1)
        return jnp.where(lane < HD, block, jnp.ones_like(block))

    def value_side(block):
        lane = lax.broadcasted_iota(jnp.int32, block.shape, 1)
        return jnp.where(lane < HD, jnp.ones_like(block), block)

    def weighted(block, weights):
        return lax.dot_general(
            block, weights, (((0,), (0,)), ((), ())), preferred_element_type=jnp.float32
        )

    tokens = token_ref[...].astype(jnp.float32).T
    natural_ref[...] = tokens.astype(jnp.bfloat16)
    rows = own_ref.shape[0]
    own_at = pl.multiple_of(lax.axis_index("kv") * rows, rows)
    own_ref[...] = natural_ref[pl.ds(own_at, rows)]
    normed = rms_scale(tokens, gain_ref[...][None]).astype(jnp.bfloat16)
    position = length + lax.broadcasted_iota(jnp.int32, (new_count, LANES), 0)
    angle = position.astype(jnp.float32) * frequency_ref[...]
    cosine = jnp.cos(angle)
    sine = jnp.sin(angle)
    lane = lax.broadcasted_iota(jnp.int32, (new_count, LANES), 1)
    sine = jnp.where(lane % HD < HD // 2, -sine, sine)

    def turned(block):
        swapped = jnp.where(
            lane % HD < HD // 2,
            pltpu.roll(block, LANES - HD // 2, 1),
            pltpu.roll(block, HD // 2, 1),
        )
        return block * cosine + swapped * sine

    key_at = lax.broadcasted_iota(jnp.int32, (new_count, columns), 0)
    query_at = lax.broadcasted_iota(jnp.int32, (new_count, columns), 1) % new_count
    causal = key_at <= query_at
    row = lax.broadcasted_iota(jnp.int32, (LANES, columns), 0)
    fresh_blocks = []
    for head in range(heads):
        qkv_copy(head).wait()
        projected = jnp.dot(
            normed,
            qkv_ref[:, head * head_width : (head + 1) * head_width],
            preferred_element_type=jnp.float32,
        )
        for pair in range(GROUP // 2):
            block = turned(projected[:, pair * LANES : (pair + 1) * LANES])
            block = (block * (HD**-0.5)).T.astype(jnp.bfloat16)
            for half in range(2):
                at = (2 * pair + half) * new_count
                query_ref[head, :HD, at : at + new_count] = block[half * HD : (half + 1) * HD]
        query_ref[head, HD:, :] = jnp.zeros((HD, columns), jnp.bfloat16)
        block = projected[:, GROUP * HD :]
        fresh_blocks.append(jnp.where(lane < HD, turned(block), block).astype(jnp.bfloat16))

    def begin(head):
        block = fresh_blocks[head]
        scores = jnp.dot(block, query_ref[head], preferred_element_type=jnp.float32)
        scores = jnp.where(causal, scores, -jnp.inf)
        sink = jnp.concatenate(
            [
                jnp.full((1, new_count), sink_ref[head * GROUP + place], jnp.float32)
                for place in range(GROUP)
            ],
            axis=1,
        )
        peak = jnp.maximum(sink, jnp.max(scores, axis=0, keepdims=True))
        weights = jnp.exp(scores - peak).astype(jnp.bfloat16)
        start = jnp.where(row < HD, jnp.exp(sink - peak), 0.0)
        total_ref[head] = start + weighted(value_side(block), weights)
        peak_ref[head : head + 1, :] = peak

    for head in range(heads):
        begin(head)
        peak = -peak_ref[head : head + 1, :]
        first = peak.astype(jnp.bfloat16).astype(jnp.float32)
        second = (peak - first).astype(jnp.bfloat16).astype(jnp.float32)
        third = peak - first - second
        tail_row = lax.broadcasted_iota(jnp.int32, (HD, columns), 0)
        shift = jnp.where(
            tail_row == 0,
            first,
            jnp.where(tail_row == 1, second, jnp.where(tail_row == 2, third, 0.0)),
        )
        query_ref[head, HD:, :] = shift.astype(jnp.bfloat16)

    def chunk_at(chunk):
        return pl.ds(pl.multiple_of(chunk * span, span), span)

    def absorb(chunk, masked):
        keys = cache_ref.at[chunk_at(chunk)]
        pltpu.make_async_copy(keys, keys, cache_sem.at[chunk]).wait()
        for head in range(heads):
            block = cache_ref[chunk_at(chunk), head * LANES : (head + 1) * LANES]
            scores = jnp.dot(
                key_side(block), query_ref[head], preferred_element_type=jnp.float32
            )
            weights = jnp.exp(scores)
            if masked:
                at = chunk * span + lax.broadcasted_iota(jnp.int32, scores.shape, 0)
                weights = jnp.where(at < length, weights, 0.0)
            total_ref[head] += weighted(value_side(block), weights.astype(jnp.bfloat16))

    def absorb_whole(chunk, _):
        absorb(chunk, False)
        return 0

    lax.fori_loop(0, whole_chunks, absorb_whole, 0)

    @pl.when(chunks > whole_chunks)
    def _():
        absorb(whole_chunks, True)

    largest = jnp.max(jnp.where(jnp.abs(total_ref[...]) < FINITE, 0.0, 1.0))

    @pl.when(largest > 0.5)
    def _():
        for head in range(heads):
            query_ref[head, HD:, :] = jnp.zeros((HD, columns), jnp.bfloat16)
        for head in range(heads):
            begin(head)

        def again(chunk, _):
            for head in range(heads):
                block = cache_ref[chunk_at(chunk), head * LANES : (head + 1) * LANES]
                scores = jnp.dot(block, query_ref[head], preferred_element_type=jnp.float32)
                at = chunk * span + lax.broadcasted_iota(jnp.int32, scores.shape, 0)
                scores = jnp.where(at < length, scores, -jnp.inf)
                old_peak = peak_ref[head : head + 1, :]
                peak = jnp.maximum(old_peak, jnp.max(scores, axis=0, keepdims=True))
                weights = jnp.exp(scores - peak).astype(jnp.bfloat16)
                total_ref[head] = total_ref[head] * jnp.exp(old_peak - peak) + weighted(
                    value_side(block), weights
                )
                peak_ref[head : head + 1, :] = peak
            return 0

        lax.fori_loop(0, chunks, again, 0)

    for head in range(heads):
        for pair in range(GROUP // 2):
            parts = []
            for half in range(2):
                at = (2 * pair + half) * new_count
                part = total_ref[head, :, at : at + new_count]
                parts.append(part[HD:] / part[0:1])
            block = jnp.concatenate(parts, axis=0).T.astype(jnp.bfloat16)
            at = head * GROUP * HD + pair * LANES
            attended_ref[:, at : at + LANES] = block
    weight_copy.wait()
    partial_ref[...] = lax.dot_general(
        attended_ref[...],
        weight_ref[...],
        (((1,), (1,)), ((), ())),
        preferred_element_type=jnp.float32,
    ).astype(jnp.bfloat16)


def attend(tokens, attn_gain, w_qkv, sink_logits, w_out, kv_cache, page_row, cached_length):
    new_count, width = tokens.shape
    heads = sink_logits.shape[0] // GROUP
    columns = GROUP * new_count
    pages, page_size, cache_width = kv_cache.shape
    frequency = THETA_BASE ** (-(np.arange(HD // 2) * 2.0 / HD))
    frequency = jnp.asarray(np.tile(frequency, 4)[None], jnp.float32)
    scalars = pl.BlockSpec(memory_space=pltpu.SMEM)
    dense = pl.BlockSpec(memory_space=pltpu.VMEM)
    apart = pl.BlockSpec(memory_space=pl.ANY)
    return pl.pallas_call(
        attend_kernel,
        in_specs=[scalars, scalars, scalars, dense, dense, dense, apart, apart, apart],
        out_specs=[dense, dense],
        out_shape=[
            jax.ShapeDtypeStruct((new_count, width), jnp.bfloat16),
            jax.ShapeDtypeStruct((new_count // lax.axis_size("kv"), width), jnp.bfloat16),
        ],
        scratch_shapes=[
            pltpu.VMEM((new_count, width), jnp.bfloat16),
            pltpu.VMEM(w_qkv.shape, jnp.bfloat16),
            pltpu.VMEM(w_out.shape[::-1], jnp.bfloat16),
            pltpu.VMEM((pages * page_size, cache_width), jnp.bfloat16),
            pltpu.VMEM((heads, LANES, columns), jnp.bfloat16),
            pltpu.VMEM((heads, LANES, columns), jnp.float32),
            pltpu.VMEM((heads, columns), jnp.float32),
            pltpu.VMEM((new_count, heads * GROUP * HD), jnp.bfloat16),
            pltpu.SemaphoreType.DMA((heads,)),
            pltpu.SemaphoreType.DMA,
            pltpu.SemaphoreType.DMA((pages // PAGE_STEP,)),
        ],
        compiler_params=pltpu.CompilerParams(vmem_limit_bytes=56 * 1024 * 1024),
        name="attend",
    )(
        page_row,
        cached_length,
        sink_logits,
        tokens.T,
        attn_gain,
        frequency,
        w_qkv,
        w_out.T,
        kv_cache,
    )


def moe_kernel(
    partial_ref,
    token_ref,
    gain_ref,
    route_ref,
    gate_ref,
    up_hbm,
    down_hbm,
    out_ref,
    up_ref,
    down_ref,
    gathered_ref,
    mixed_ref,
    mate_ref,
    plane_ref,
    column_ref,
    share_ref,
    pair_ref,
    cross_ref,
    residual_ref,
    hidden_ref,
    tail_ref,
    up_sem,
    down_sem,
    share_sem,
    cross_sem,
    gather_sem,
    gather_mate_sem,
    other_sem,
    mate_sem,
    plane_sem,
    column_sem,
    sent_sem,
    *,
    grid_z,
    grid_y,
    grid_x,
):
    req, kv = lax.axis_index("req"), lax.axis_index("kv")
    kv_count = 2 * grid_x
    z, y = req // grid_y, req % grid_y
    x, core = kv // 2, kv % 2
    blocks, rows, width = mixed_ref.shape
    last_tile = width // 128 * 128
    experts = up_hbm.shape[0]
    plane_blocks = grid_y * kv_count
    xs, ys = range(1, grid_x), range(1, grid_y)

    def at_kv(other):
        return (req, other)

    mate = at_kv(2 * x + 1 - core)

    def x_peer(step):
        return at_kv(2 * ((x + step) % grid_x) + core)

    def y_peer(step):
        return (z * grid_y + (y + step) % grid_y, kv)

    def z_peer(step):
        return (((z + step) % grid_z) * grid_y + y, kv)

    def origin(plane):
        return (z + grid_z - plane) % grid_z

    def block_at(plane, y_step, x_step, parity):
        row = origin(plane) * grid_y + (y + grid_y + y_step) % grid_y
        return row * kv_count + 2 * ((x + grid_x + x_step) % grid_x) + parity

    def remote(source, target, sent, received, device):
        return pltpu.make_async_remote_copy(
            src_ref=source,
            dst_ref=target,
            send_sem=sent,
            recv_sem=received,
            device_id=device,
            device_id_type=pl.DeviceIdType.MESH,
        )

    def arrived(block, received):
        pltpu.make_async_copy(block, block, received).wait()

    up_copies = [
        pltpu.make_async_copy(up_hbm.at[e], up_ref.at[e], up_sem.at[e]) for e in range(experts)
    ]
    down_copies = [
        pltpu.make_async_copy(down_hbm.at[e], down_ref.at[e], down_sem.at[e])
        for e in range(experts)
    ]
    for expert in range(experts):
        up_copies[expert].start()
        down_copies[expert].start()

    tail_width = gathered_ref.shape[2] - last_tile
    lead = width - last_tile
    every_expert = experts * (blocks // kv_count)
    expert_at = lax.broadcasted_iota(jnp.int32, (tail_width, gate_ref.shape[1]), 0) - lead
    upper_side = expert_at < every_expert
    expert_at = jnp.where(upper_side, expert_at, expert_at - every_expert)
    tail = jnp.zeros(expert_at.shape, jnp.float32)
    for turn in range(gate_ref.shape[0]):
        named = expert_at == route_ref[turn : turn + 1, :]
        tail = jnp.where(named, gate_ref[turn : turn + 1, :], tail)
    upper = tail.astype(jnp.bfloat16).astype(jnp.float32)
    tail_ref[...] = jnp.where(upper_side, upper, tail - upper).T.astype(jnp.bfloat16)

    barrier = pltpu.get_barrier_semaphore()
    partners = [at_kv((kv + step) % kv_count) for step in range(1, kv_count)]
    partners += [y_peer(step) for step in ys] + [z_peer(step) for step in range(1, grid_z)]
    for device in partners:
        pl.semaphore_signal(
            barrier, inc=1, device_id=device, device_id_type=pl.DeviceIdType.MESH
        )
    pl.semaphore_wait(barrier, len(partners))

    def row_block(index):
        return pl.ds(pl.multiple_of(index * rows, rows), rows)

    for step in list(xs) + [0]:
        column = (x + step) % grid_x
        remote(
            partial_ref.at[row_block(2 * column + 1 - core)],
            share_ref.at[step],
            sent_sem.at[0],
            share_sem.at[step],
            mate,
        ).start()
    for step in xs:
        arrived(share_ref.at[step], share_sem.at[step])
        pair = partial_ref[row_block(2 * ((x + step) % grid_x) + core)].astype(jnp.float32)
        pair += share_ref[step].astype(jnp.float32)
        pair_ref[step - 1] = pair.astype(jnp.bfloat16)
        remote(
            pair_ref.at[step - 1],
            cross_ref.at[step - 1],
            sent_sem.at[3],
            cross_sem.at[step - 1],
            x_peer(step),
        ).start()
    arrived(share_ref.at[0], share_sem.at[0])
    summed = partial_ref[row_block(kv)].astype(jnp.float32) + share_ref[0].astype(jnp.float32)
    for step in xs:
        arrived(cross_ref.at[step - 1], cross_sem.at[step - 1])
        summed += cross_ref[step - 1].astype(jnp.float32)
    residual = token_ref[...].astype(jnp.float32) + summed
    residual_ref[...] = residual
    own = block_at(0, 0, 0, core)
    gathered_ref[own, :, last_tile:] = tail_ref[row_block(kv)]
    gathered_ref[own, :, :width] = rms_scale(residual, gain_ref[...][None]).astype(jnp.bfloat16)

    middle = width // 256 * 128
    halves = (slice(0, middle), slice(middle, gathered_ref.shape[2]))

    def pass_on(block, received, device, part=None):
        ref = gathered_ref.at[block]
        if part is not None:
            ref = gathered_ref.at[block, :, part]
        remote(ref, ref, sent_sem.at[1], received, device).start()

    def gather_own(plane):
        block = block_at(plane, 0, 0, core)

        @pl.when(plane > 0)
        def _():
            arrived(gathered_ref.at[block], gather_sem.at[plane, 0, 0])

        for j in xs:
            pass_on(block, gather_sem.at[plane, 0, j], x_peer(j))
        for i in ys:
            pass_on(block, gather_sem.at[plane, i, 0], y_peer(i))
        pass_on(block, gather_mate_sem.at[plane, 0, 0], mate)

        @pl.when(plane + 1 < grid_z)
        def _():
            pass_on(block, gather_sem.at[plane + 1, 0, 0], z_peer(1))

    def gather_near(plane):
        def take(i, j):
            block = block_at(plane, -i, -j, core)
            arrived(gathered_ref.at[block], gather_sem.at[plane, i, j])
            return block

        near_y = [take(i, 0) for i in ys]
        for i, block in zip(ys, near_y):
            for j in xs:
                pass_on(block, gather_sem.at[plane, i, j], x_peer(j), halves[0])
        near_x = [take(0, j) for j in xs]
        for j, block in zip(xs, near_x):
            for i in ys:
                pass_on(block, other_sem.at[plane, i, j], y_peer(i), halves[1])
        for i, block in zip(ys, near_y):
            pass_on(block, gather_mate_sem.at[plane, i, 0], mate)
        for j, block in zip(xs, near_x):
            pass_on(block, gather_mate_sem.at[plane, 0, j], mate)

    def gather_far(plane):
        for i in ys:
            for j in xs:
                block = block_at(plane, -i, -j, core)
                arrived(gathered_ref.at[block, :, halves[0]], gather_sem.at[plane, i, j])
                arrived(gathered_ref.at[block, :, halves[1]], other_sem.at[plane, i, j])
                pass_on(block, gather_mate_sem.at[plane, i, j], mate)

    def gather_last(plane):
        for i in range(grid_y):
            for j in range(grid_x):
                block = block_at(plane, -i, -j, 1 - core)
                arrived(gathered_ref.at[block], gather_mate_sem.at[plane, i, j])

    def raise_up(plane, expert):
        start = pl.multiple_of(origin(plane) * plane_blocks, plane_blocks)
        part = gathered_ref[pl.ds(start, plane_blocks), :, :width]
        part = part.reshape(plane_blocks * rows, width)

        def projected(which):
            return lax.dot_general(
                part,
                up_ref[expert, which],
                (((1,), (1,)), ((), ())),
                preferred_element_type=jnp.float32,
            )

        gate, up = projected(0), projected(1)
        gates = gathered_ref[pl.ds(start, plane_blocks), :, last_tile:].reshape(-1, 128)
        place = width - last_tile + req * experts + expert
        lane = lax.broadcasted_iota(jnp.int32, gates.shape, 1)
        choice = (lane == place) | (lane == place + experts * (blocks // kv_count))
        weight = jnp.sum(
            jnp.where(choice, gates.astype(jnp.float32), 0.0), axis=1, keepdims=True
        )
        hidden = gate * jax.nn.sigmoid(ALPHA_GLU * gate) * (up + 1.0) * weight
        hidden_ref[expert] = hidden.astype(jnp.bfloat16)

    sum_halves = (slice(0, middle), slice(middle, width))

    def hand_over(source, target, received, device):
        remote(source, target, sent_sem.at[2], received, device).start()

    def add_to(block, part, terms):
        value = mixed_ref[block, :, part].astype(jnp.float32)
        for term in terms:
            value += term[...].astype(jnp.float32)
        mixed_ref[block, :, part] = value.astype(jnp.bfloat16)

    far = [(i, j) for i in ys for j in xs]
    side_x = [(0, j) for j in xs]
    side_y = [(i, 0) for i in ys]

    def lower(plane):
        start = pl.multiple_of(origin(plane) * plane_blocks, plane_blocks)
        for turn, part in enumerate(sum_halves):
            mixed = jnp.dot(
                hidden_ref[0], down_ref[0, :, part], preferred_element_type=jnp.float32
            )
            for expert in range(1, experts):
                mixed += jnp.dot(
                    hidden_ref[expert],
                    down_ref[expert, :, part],
                    preferred_element_type=jnp.float32,
                )
            mixed_ref[pl.ds(start, plane_blocks), :, part] = mixed.astype(jnp.bfloat16).reshape(
                plane_blocks, rows, part.stop - part.start
            )
            for i, j in far + side_x + side_y + [(0, 0)]:
                hand_over(
                    mixed_ref.at[block_at(plane, i, j, 1 - core), :, part],
                    mate_ref.at[plane, i, j, :, part],
                    mate_sem.at[turn, plane, i, j],
                    mate,
                )

    def plane_send(plane, i, j, turn, device):
        part = sum_halves[turn]
        hand_over(
            mixed_ref.at[block_at(plane, i, j, core), :, part],
            plane_ref.at[plane, i, j, :, part],
            plane_sem.at[turn, plane, i, j],
            device,
        )

    def plane_take(plane, i, j, turn):
        part = sum_halves[turn]
        arrived(plane_ref.at[plane, i, j, :, part], plane_sem.at[turn, plane, i, j])
        return plane_ref.at[plane, i, j, :, part]

    def sum_mate(plane):
        for turn, part in enumerate(sum_halves):
            for i, j in far + (side_y + side_x if turn else side_x + side_y) + [(0, 0)]:
                term = mate_ref.at[plane, i, j, :, part]
                arrived(term, mate_sem.at[turn, plane, i, j])
                add_to(block_at(plane, i, j, core), part, [term])
                if j and turn == 0:
                    plane_send(plane, i, j, 0, x_peer(j))
                if i and turn == 1:
                    plane_send(plane, i, j, 1, y_peer(i))

    def sum_near(plane):
        for i in ys:
            terms = [plane_take(plane, i, j, 0) for j in xs]
            add_to(block_at(plane, i, 0, core), sum_halves[0], terms)
            plane_send(plane, i, 0, 0, y_peer(i))
        for j in xs:
            terms = [plane_take(plane, i, j, 1) for i in ys]
            add_to(block_at(plane, 0, j, core), sum_halves[1], terms)
            plane_send(plane, 0, j, 1, x_peer(j))
        terms = [plane_take(plane, 0, j, 0) for j in xs]
        add_to(block_at(plane, 0, 0, core), sum_halves[0], terms)
        terms = [plane_take(plane, i, 0, 1) for i in ys]
        add_to(block_at(plane, 0, 0, core), sum_halves[1], terms)

    def sum_far(plane):
        block = block_at(plane, 0, 0, core)
        add_to(block, sum_halves[0], [plane_take(plane, i, 0, 0) for i in ys])
        add_to(block, sum_halves[1], [plane_take(plane, 0, j, 1) for j in xs])

        for step in range(1, grid_z):

            @pl.when(plane == step)
            def _():
                hand_over(
                    mixed_ref.at[block],
                    column_ref.at[step - 1],
                    column_sem.at[step - 1],
                    z_peer(grid_z - step),
                )

    turns = experts * grid_z

    def run_at(turn, first, task, start=0):
        shifted = turn - first

        @pl.when(
            (shifted >= experts * start) & (shifted < turns) & (shifted % experts == 0)
        )
        def _():
            task(shifted // experts)

    gather_own(0)
    gather_near(0)
    if grid_z > 1:
        gather_own(1)
    gather_far(0)

    def advance(turn, _):
        run_at(turn, 6, sum_far)
        run_at(turn, 5, sum_near)
        run_at(turn, 0, gather_last)
        run_at(turn, -4, gather_own, 2)

        @pl.when(turn == 1)
        def _():
            gather_near(1)

        run_at(turn, -1, gather_far, 2)
        run_at(turn, 3, sum_mate)
        for expert in range(experts):

            @pl.when(turn == expert)
            def _():
                up_copies[expert].wait()
                down_copies[expert].wait()

        @pl.when(turn < turns)
        def _():
            raise_up(turn // experts, turn % experts)

        run_at(turn, -3, gather_near, 2)

        @pl.when(turn == 1)
        def _():
            gather_far(1)


        @pl.when((turn < turns) & (turn % experts == experts - 1))
        def _():
            lower(turn // experts)

        return 0

    lax.fori_loop(0, 5 + turns, advance, 0)

    result = residual_ref[...] + mixed_ref[own].astype(jnp.float32)
    for step in range(1, grid_z):
        arrived(column_ref.at[step - 1], column_sem.at[step - 1])
        result += column_ref[step - 1].astype(jnp.float32)
    out_ref[...] = result.astype(jnp.bfloat16)
    arrived(share_ref, sent_sem.at[0])
    arrived(pair_ref, sent_sem.at[3])
    arrived(gathered_ref.at[: blocks - 1], sent_sem.at[1])
    arrived(mixed_ref.at[: blocks - 1], sent_sem.at[2])


def mixture(partial_out, tokens, moe_gain, routes, gate_weights, w_gate_up, w_down):
    kv_count, req_count = lax.axis_size("kv"), lax.axis_size("req")
    new_count, width = partial_out.shape
    rows = new_count // kv_count
    experts, hidden = w_down.shape[:2]
    blocks = kv_count * req_count
    grid_x = kv_count // 2
    grid_z = 4 if req_count % 4 == 0 else req_count
    grid_y = req_count // grid_z
    dense = pl.BlockSpec(memory_space=pltpu.VMEM)
    apart = pl.BlockSpec(memory_space=pl.ANY)
    half = jnp.bfloat16
    last_tile = width // 128 * 128
    tail_width = width - last_tile + 2 * experts * req_count
    full_width = last_tile + tail_width + -tail_width % 128
    return pl.pallas_call(
        functools.partial(moe_kernel, grid_z=grid_z, grid_y=grid_y, grid_x=grid_x),
        in_specs=[dense, dense, dense, dense, dense, apart, apart],
        out_specs=dense,
        out_shape=jax.ShapeDtypeStruct((rows, width), half),
        scratch_shapes=[
            pltpu.VMEM((experts, 2, hidden, width), half),
            pltpu.VMEM(w_down.shape, half),
            pltpu.VMEM((blocks, rows, full_width), half),
            pltpu.VMEM((blocks, rows, width), half),
            pltpu.VMEM((grid_z, grid_y, grid_x, rows, width), half),
            pltpu.VMEM((grid_z, grid_y, grid_x, rows, width), half),
            pltpu.VMEM((grid_z - 1, rows, width), half),
            pltpu.VMEM((grid_x, rows, width), half),
            pltpu.VMEM((grid_x - 1, rows, width), half),
            pltpu.VMEM((grid_x - 1, rows, width), half),
            pltpu.VMEM((rows, width), jnp.float32),
            pltpu.VMEM((experts, blocks // grid_z * rows, hidden), half),
            pltpu.VMEM((new_count, full_width - last_tile), half),
            pltpu.SemaphoreType.DMA((experts,)),
            pltpu.SemaphoreType.DMA((experts,)),
            pltpu.SemaphoreType.DMA((grid_x,)),
            pltpu.SemaphoreType.DMA((grid_x - 1,)),
            pltpu.SemaphoreType.DMA((grid_z, grid_y, grid_x)),
            pltpu.SemaphoreType.DMA((grid_z, grid_y, grid_x)),
            pltpu.SemaphoreType.DMA((grid_z, grid_y, grid_x)),
            pltpu.SemaphoreType.DMA((2, grid_z, grid_y, grid_x)),
            pltpu.SemaphoreType.DMA((2, grid_z, grid_y, grid_x)),
            pltpu.SemaphoreType.DMA((grid_z - 1,)),
            pltpu.SemaphoreType.DMA((4,)),
        ],
        compiler_params=pltpu.CompilerParams(
            vmem_limit_bytes=63 * 1024 * 1024, collective_id=0, has_side_effects=True
        ),
        name="mixture",
    )(
        partial_out,
        tokens,
        moe_gain,
        routes.T,
        gate_weights.T,
        jnp.swapaxes(w_gate_up, 2, 3),
        w_down,
    )


def on_device(
    tokens,
    attn_gain,
    w_qkv,
    sink_logits,
    w_out,
    kv_cache,
    page_table,
    cache_lengths,
    moe_gain,
    routes,
    gate_weights,
    w_gate_up,
    w_down,
):
    partial_out, own_tokens = attend(
        tokens[0],
        attn_gain,
        w_qkv,
        sink_logits,
        w_out,
        kv_cache,
        page_table[0],
        cache_lengths,
    )
    return mixture(
        partial_out, own_tokens, moe_gain, routes[0], gate_weights[0], w_gate_up, w_down
    )[None]


def solution(mesh):
    in_specs = (
        P("req", None, None),
        P(),
        P(None, "kv"),
        P("kv"),
        P("kv", None),
        P("req", None, "kv"),
        P("req", None),
        P("req"),
        P(),
        P("req", None, None),
        P("req", None, None),
        P("req", None, None, "kv"),
        P("req", "kv", None),
    )
    out_specs = P("req", "kv", None)
    return jax.shard_map(
        on_device, mesh=mesh, in_specs=in_specs, out_specs=out_specs, check_vma=False
    )
```
